128 devices in a mesh: facet: 8 (over z, core), vis: 16 (over y, x).
Axes of the slice: x: 4, y: 4, z: 4, core: 2. Of those that a mesh axis runs over, the one named last changes fastest.
Arguments:
- model: bfloat16 [2048, 2048], P(('facet', 'vis')), may hold values from -0.005859375 to 0.005859375
- observed: bfloat16 [1024, 2, 128, 128], P(('facet', 'vis')), may hold values from -6 to 6
- u_offsets: int32 [1024], P(('facet', 'vis')), may hold values from 0 to 32767
- v_offsets: int32 [1024], P(('facet', 'vis')), may hold values from 0 to 32767
- facet_lists: int32 [1024, 2], P(('facet', 'vis')), may hold values from 0 to 7, all different within a row; in each aligned block of 8 rows (0 to 7, 8 to 15, ...) at most 2 rows name the same one
Outputs:
- dirty: float32 [2048, 2048], P(('facet', 'vis'))
- residual: bfloat16 [1024, 2, 128, 128], P(('facet', 'vis'))
The draws below stay inside these ranges and needn't reach their ends.
Inputs may be any that keep to these rules, and one draw needn't show every extreme that they name: `facet_lists`: each row names 2 different facets; among the 8 subgrids of one device no facet is named more than 2 times, and that many is reached.
All inputs are finite; a program needn't handle non-finite values.
Results may differ from the reference program's by a relative error of at most 0.018.
Values may be sent and summed in bfloat16 or wider, within the bound.
A program may use at most 128 MiB of HBM per device.

```python
import math
import jax
import jax.numpy as jnp
import numpy as np
from jax import lax

IMG = 32768
FW = 2048
S = 128
TOPF = 2
G_DEV = 8
FRT = 256
NR = 2048
NSUB = 1024
CAP = 2
N_FACET = 8


def with_ends(entries, rng, least, high):
    dims = entries.shape
    place = [jax.random.randint(jax.random.fold_in(rng, axis), (), 0, dims[axis]) for axis in range(len(dims))]
    entries = entries.at[tuple(place)].set(least)
    longest = dims.index(max(dims))
    place[longest] = (place[longest] + 1) % dims[longest]
    return entries.at[tuple(place)].set(high)


def level_of(rng, extent, cuts, low, high):
    factor_of, own = 1.0, jax.random.fold_in(rng, 6)
    for axis_at, blocks in cuts:
        draws = jnp.exp(jax.random.uniform(jax.random.fold_in(own, axis_at), (blocks,), jnp.float32, low / len(cuts), high / len(cuts)))
        factor_of = factor_of * jnp.repeat(draws, extent[axis_at] // blocks).reshape([-1 if axis == axis_at else 1 for axis in range(len(extent))])
    return factor_of


def deal_out(key, own, number, rows, count, top, reach, slope):
    order = jax.random.permutation(key, count)
    heavy_load, common = load_shares(count, rows * top, reach, slope, True), load_shares(count, rows * top, reach, slope, False)
    places = jnp.arange(count)

    def named(tallies, rotation):
        used = int((tallies > 0).sum())
        fixed = max(1, used // 4)
        passed = fixed + (places - fixed + rotation * (used - fixed)) % max(1, count - fixed)
        return jnp.zeros((count,), jnp.int32).at[order[jnp.where(places < fixed, places, passed)]].set(jnp.asarray(tallies, jnp.int32))

    tallies = jnp.where(number % 4 == 0, named(heavy_load, number // 4), named(common, number - number // 4 - 1))
    mixed = jax.random.permutation(jax.random.fold_in(own, 3), count)
    giver, taker = mixed[0:count // 2 * 2:2], mixed[1:count // 2 * 2:2]
    slack = jnp.minimum(tallies[giver] - 1, reach - tallies[taker]) // 2
    slack = jnp.where((giver == order[0]) | (taker == order[0]) | (tallies[taker] == 0), 0, jnp.maximum(slack, 0))
    passed = jax.random.randint(jax.random.fold_in(own, 4), (count // 2,), 0, 1 << 20) % (slack + 1)
    tallies = tallies.at[giver].add(-passed).at[taker].add(passed)
    items = jnp.searchsorted(jnp.cumsum(tallies), jnp.arange(rows * top), side="right").astype(jnp.int32)
    listing = items.reshape(top, rows).T
    listing = listing[jax.random.permutation(jax.random.fold_in(own, 1), rows)]
    rotation = jax.random.randint(jax.random.fold_in(own, 2), (rows, 1), 0, top)
    return jnp.take_along_axis(listing, (jnp.arange(top)[None, :] + rotation) % top, axis=1)


def load_shares(amount, total, bound, skew, full):
    portions = [(1 << 20) // math.isqrt(rank ** skew) + 1 for rank in range(1, amount + 1)]
    largest = bound if full else min(bound, max(-(-total // amount), total * portions[0] // sum(portions)))
    least = 1 if total - largest >= amount - 1 else 0
    holding, surplus = [largest] + [least] * (amount - 1), total - largest - least * (amount - 1)
    while surplus > 0:
        candidates = [i for i in range(1, amount) if holding[i] < largest] or [i for i in range(1, amount) if holding[i] < bound]
        pool, budget = sum([portions[i] for i in candidates]), surplus
        for i in candidates:
            extra = min(bound - holding[i], max(1, budget * portions[i] // pool), surplus)
            holding[i] = holding[i] + extra
            surplus = surplus - extra
    return np.array(holding)


def centred(own_key, extent, deviation, reach, split=(), kind=jnp.bfloat16):
    values = deviation * jax.random.normal(own_key, extent, jnp.float32)
    if split:
        values = values * level_of(own_key, extent, split, -0.22, 0.18)
    return jnp.clip(values, -reach, reach).astype(kind)


def setup_inputs(seed: int = 0) -> dict:
    keys = jax.random.split(jax.random.key(seed), 6)
    model = centred(keys[0], (NR, FW), (FRT * FW * TOPF) ** -0.5, 0.005859375, ((0, 128),))
    observed = centred(keys[1], (NSUB, 2, S, S), 1.0, 6.0, ((0, 128),))
    u_offsets = with_ends(jax.random.randint(keys[2], (NSUB,), 0, IMG), jax.random.fold_in(keys[2], 1), 0, IMG - 1).astype(jnp.int32)
    v_offsets = with_ends(jax.random.randint(keys[3], (NSUB,), 0, IMG), jax.random.fold_in(keys[3], 1), 0, IMG - 1).astype(jnp.int32)
    facet_lists_keys = jax.random.split(jax.random.fold_in(keys[4], 1), NSUB // G_DEV)
    facet_lists_turns = jax.random.permutation(jax.random.fold_in(keys[4], 3), NSUB // G_DEV)
    facet_lists = jax.vmap(lambda own, number: deal_out(jax.random.fold_in(keys[4], 2), own, number, G_DEV, N_FACET, TOPF, CAP, 2))(facet_lists_keys, facet_lists_turns).reshape((NSUB, TOPF))
    return dict(model=model, observed=observed, u_offsets=u_offsets, v_offsets=v_offsets, facet_lists=facet_lists)


two_pi = 6.283185307179586


def phase_table(offsets, length, coords, period):
    steps = offsets[..., None] + jnp.arange(length, dtype=jnp.int32)
    index = (steps[..., :, None] * coords[..., None, :]) % period
    angle = index.astype(jnp.float32) * jnp.float32(two_pi / period)
    return jnp.cos(angle).astype(jnp.bfloat16), jnp.sin(angle).astype(jnp.bfloat16)


def reference(model, observed, u_offsets, v_offsets, facet_lists):
    facet_step = IMG // N_FACET
    local = jnp.arange(FRT, dtype=jnp.int32)
    column_count = jnp.arange(FW, dtype=jnp.int32)
    f32 = jnp.float32

    def one_subgrid(dirty, item):
        observed_one, u_one, v_one, listed = item
        coords = listed[:, None] * facet_step + local[None, :]
        cos_u, sin_u = phase_table(jnp.broadcast_to(u_one, (TOPF,)), S, coords, IMG)
        cos_v, sin_v = phase_table(v_one, S, column_count, IMG)
        chosen = jnp.stack([lax.dynamic_slice_in_dim(model, (listed[which] * FRT).astype(jnp.int32), FRT, 0) for which in range(TOPF)])
        w_real = jnp.einsum("kax,kxy->kay", cos_u.astype(f32), chosen.astype(f32)).astype(jnp.bfloat16)
        w_imag = (-jnp.einsum("kax,kxy->kay", sin_u.astype(f32), chosen.astype(f32))).astype(jnp.bfloat16)
        p_real = jnp.einsum("kay,by->ab", w_real.astype(f32), cos_v.astype(f32)) + jnp.einsum("kay,by->ab", w_imag.astype(f32), sin_v.astype(f32))
        predicted_imaginary = jnp.einsum("kay,by->ab", w_imag.astype(f32), cos_v.astype(f32)) - jnp.einsum("kay,by->ab", w_real.astype(f32), sin_v.astype(f32))
        res_real = (observed_one[0].astype(f32) - p_real).astype(jnp.bfloat16)
        res_imag = (observed_one[1].astype(f32) - predicted_imaginary).astype(jnp.bfloat16)
        row_real = (jnp.einsum("kax,ab->kxb", cos_u.astype(f32), res_real.astype(f32)) - jnp.einsum("kax,ab->kxb", sin_u.astype(f32), res_imag.astype(f32))).astype(jnp.bfloat16)
        row_imag = (jnp.einsum("kax,ab->kxb", cos_u.astype(f32), res_imag.astype(f32)) + jnp.einsum("kax,ab->kxb", sin_u.astype(f32), res_real.astype(f32))).astype(jnp.bfloat16)
        terms = jnp.einsum("kxb,by->kxy", row_real.astype(f32), cos_v.astype(f32)) - jnp.einsum("kxb,by->kxy", row_imag.astype(f32), sin_v.astype(f32))
        for which in range(TOPF):
            start = (listed[which] * FRT).astype(jnp.int32)
            before = lax.dynamic_slice_in_dim(dirty, start, FRT, 0)
            dirty = lax.dynamic_update_slice_in_dim(dirty, before + terms[which], start, 0)
        return dirty, jnp.stack([res_real, res_imag])

    start_image = jnp.zeros((NR, FW), jnp.float32)
    dirty, residual = lax.scan(one_subgrid, start_image, (observed, u_offsets, v_offsets, facet_lists))
    return dirty * (1.0 / (S * S)), residual
```

```python
import math

import jax
import jax.numpy as jnp
from jax import lax
from jax.experimental import pallas as pl
from jax.experimental.pallas import tpu as pltpu
from jax.sharding import PartitionSpec as P

IMG = 32768
LANES = 128
NF = 8
NV = 16
S = 128
FW = 2048
FRT = 256
ROWS = 16
G = 8
YC = FW // LANES
XC = FRT // LANES
STEP = IMG // NF
MESH = pl.DeviceIdType.MESH
F32 = jnp.float32
BF16 = jnp.bfloat16
NT = (((1,), (1,)), ((), ()))
NN = (((1,), (0,)), ((), ()))


def sincos(index):
    quarter = (index + IMG // 8) >> 13
    rest = index - (quarter << 13)
    angle = rest.astype(F32) * F32(2.0 * math.pi / IMG)
    t = angle * angle
    sn = angle * (1.0 + t * (-1.0 / 6 + t * (1.0 / 120 + t * (-1.0 / 5040 + t * (1.0 / 362880)))))
    cs = 1.0 + t * (-0.5 + t * (1.0 / 24 + t * (-1.0 / 720 + t * (1.0 / 40320))))
    odd = (quarter & 1) == 1
    c = jnp.where(odd, sn, cs)
    s = jnp.where(odd, cs, sn)
    c = jnp.where(((quarter + 1) & 2) != 0, -c, c)
    s = jnp.where((quarter & 2) != 0, -s, s)
    return c, s


def iota(shape, axis):
    return lax.broadcasted_iota(jnp.int32, shape, axis)


def kernel(
    model, observed, u_off, v_off, lists, dirty, residual,
    image, uv_out, uv_in, e_c, e_s, g_c, g_s, pv_c, pv_s, pu_c, pu_s, cv, cu, cut,
    p_out, p_in, r_out, r_in, total, d_out, d_in,
    ag_ss, ag_rs, uv_ss, uv_rs, p_ss, p_rs, r_ss, r_rs, d_ss, d_rs,
):
    f = lax.axis_index("facet")
    j = lax.axis_index("vis")

    def other_facet(h):
        return {"facet": h, "vis": j}

    def other_vis(k):
        return {"facet": f, "vis": k}

    barrier = pltpu.get_barrier_semaphore()
    for d in range(1, NV):
        pl.semaphore_signal(barrier, inc=1, device_id=other_vis(lax.rem(j + d, NV)), device_id_type=MESH)
    for d in range(1, NF):
        pl.semaphore_signal(barrier, inc=1, device_id=other_facet(lax.rem(f + d, NF)), device_id_type=MESH)
    pl.semaphore_wait(barrier, NV - 1 + NF - 1)

    def remote(src, dst, ss, rs, device):
        return pltpu.make_async_remote_copy(
            src_ref=src, dst_ref=dst, send_sem=ss, recv_sem=rs, device_id=device, device_id_type=MESH
        )

    def ag_copy(sender, target):
        return remote(
            model, image.at[pl.ds(pl.multiple_of(sender * ROWS, ROWS), ROWS), :],
            ag_ss.at[target], ag_rs.at[sender], other_vis(target),
        )

    first, last = [], []
    hits = [[lists[g, k] for k in range(2)] for g in range(G)]
    for h in range(NF):
        lo, hi = jnp.int32(0), jnp.int32(0)
        for g in range(G):
            named = (hits[g][0] == h) | (hits[g][1] == h)
            hi = jnp.where(named, g, hi)
        for g in reversed(range(G)):
            named = (hits[g][0] == h) | (hits[g][1] == h)
            lo = jnp.where(named, g, lo)
        first.append(lo)
        last.append(hi)

    row = iota((8, LANES), 0)
    for h in range(NF):
        a, b = first[h], last[h]
        uv_out[h] = jnp.where(
            row == 0, u_off[a], jnp.where(row == 1, u_off[b], jnp.where(row == 2, v_off[a], v_off[b]))
        )

    def uv_copy(sender, target):
        return remote(uv_out.at[target], uv_in.at[sender], uv_ss.at[target], uv_rs.at[sender], other_facet(target))

    def far_first(i):
        q = i // 2
        dz = jnp.where(q == 0, 2, jnp.where(q == 1, 1, jnp.where(q == 2, 3, 0)))
        z = lax.rem(f // 2 + dz, 4)
        c = lax.rem(lax.rem(f, 2) + 1 + lax.rem(i, 2), 2)
        return z * 2 + c

    @pl.loop(0, NF - 1)
    def _(i):
        uv_copy(f, far_first(i)).start()

    @pl.loop(1, NV)
    def _(d):
        ag_copy(j, lax.rem(j + d, NV)).start()

    image[pl.ds(pl.multiple_of(j * ROWS, ROWS), ROWS), :] = model[...]
    uv_in[f] = uv_out[f]

    lane = iota((S, LANES), 1)
    sub = iota((S, LANES), 0)

    @pl.loop(0, YC)
    def _(r):
        c, s = sincos((sub * (r * LANES + lane)) & (IMG - 1))
        e_c[r] = c
        e_s[r] = s

    @pl.loop(0, XC)
    def _(r):
        c, s = sincos((sub * (f * STEP + r * LANES + lane)) & (IMG - 1))
        g_c[r] = c
        g_s[r] = s

    @pl.loop(0, NF - 1)
    def _(i):
        uv_copy(far_first(i), far_first(i)).wait_recv()

    y_of = iota((YC, LANES), 0) * LANES + iota((YC, LANES), 1)
    x_of = iota((8, LANES), 0) * LANES + iota((8, LANES), 1) + f * STEP

    @pl.loop(0, NF)
    def _(h):
        for s in range(2):
            u = uv_in[h, s : s + 1, :]
            v = uv_in[h, 2 + s : 3 + s, :]
            c, sn = sincos((v * y_of) & (IMG - 1))
            pv_c[2 * h + s] = c
            pv_s[2 * h + s] = sn
            c, sn = sincos((u * x_of) & (IMG - 1))
            pu_c[2 * h + s] = c
            pu_s[2 * h + s] = sn

    @pl.loop(0, 2 * NF)
    def _(n):
        @pl.loop(0, YC)
        def _(r):
            pc = pv_c[n, pl.ds(r, 1), :]
            ps = pv_s[n, pl.ds(r, 1), :]
            ec, es = e_c[r], e_s[r]
            at = pl.ds(pl.multiple_of(r * LANES, LANES), LANES)
            cv[n, 0:S, at] = (pc * ec - ps * es).astype(BF16)
            cv[n, S : 2 * S, at] = (ps * ec + pc * es).astype(BF16)

        for r in range(XC):
            pc = pu_c[n, r : r + 1, :]
            ps = pu_s[n, r : r + 1, :]
            ec, es = g_c[r], g_s[r]
            at = slice(r * LANES, (r + 1) * LANES)
            c = pc * ec - ps * es
            s = ps * ec + pc * es
            cu[n, 0:S, at] = c.astype(BF16)
            cu[n, S : 2 * S, at] = s.astype(BF16)
            cut[n, at, 0:S] = c.T.astype(BF16)
            cut[n, at, S : 2 * S] = s.T.astype(BF16)

    @pl.loop(1, NV)
    def _(d):
        k = lax.rem(j + d, NV)
        ag_copy(k, k).wait_recv()

    def predict(h):
        for s in range(2):
            n = 2 * h + s
            t = lax.dot_general(cv[n], image[...], NT, preferred_element_type=F32).astype(BF16)
            o = lax.dot_general(cu[n], t, NT, preferred_element_type=F32)
            yield s, (o[0:S, 0:S] - o[S:, S:]).astype(BF16), (-(o[S:, 0:S] + o[0:S, S:])).astype(BF16)

    def p_copy(sender, target):
        return remote(
            p_out.at[target], p_in.at[pl.ds(2 * sender, 2)], p_ss.at[target], p_rs.at[sender], other_facet(target)
        )

    @pl.loop(0, NF)
    def _(i):
        h = far_first(i)
        for s, re, im in predict(h):
            p_out[h, s, 0] = re
            p_out[h, s, 1] = im

        @pl.when(i < NF - 1)
        def _():
            p_copy(f, h).start()

    for s in range(2):
        p_in[2 * f + s] = p_out[f, s]

    @pl.loop(0, NF - 1)
    def _(i):
        p_copy(far_first(i), far_first(i)).wait_recv()

    for g in range(G):
        acc = observed[g].astype(F32)
        for k in range(2):
            h = hits[g][k]
            slot = jnp.int32(0)
            for e in range(g):
                slot = jnp.where((hits[e][0] == h) | (hits[e][1] == h), 1, slot)
            acc = acc - p_in[2 * h + slot].astype(F32)
        residual[g] = acc.astype(BF16)

    def r_copy(sender, target):
        return remote(
            r_out.at[pl.ds(2 * target, 2)], r_in.at[pl.ds(2 * sender, 2)],
            r_ss.at[target], r_rs.at[sender], other_facet(target),
        )

    for h in range(NF):
        r_out[2 * h] = residual[first[h]]
        r_out[2 * h + 1] = residual[last[h]]

    @pl.loop(0, NF - 1)
    def _(i):
        r_copy(f, far_first(i)).start()

    for s in range(2):
        r_in[2 * f + s] = r_out[2 * f + s]

    total[...] = jnp.zeros_like(total)

    @pl.loop(0, NF)
    def _(i):
        h = far_first(NF - 1 - i)

        @pl.when(i > 0)
        def _():
            r_copy(h, h).wait_recv()

        for s in range(2):
            n = 2 * h + s
            re = r_in[n, 0]
            im = r_in[n, 1]
            top = jnp.concatenate([re, -im], axis=1)
            bottom = jnp.concatenate([-im, -re], axis=1)
            both = jnp.concatenate([top, bottom], axis=0)
            z = lax.dot_general(cut[n], both, NN, preferred_element_type=F32).astype(BF16)
            total[...] += lax.dot_general(z, cv[n], NN, preferred_element_type=F32)

    def d_copy(sender, target):
        return remote(d_out.at[target], d_in.at[sender], d_ss.at[target], d_rs.at[sender], other_vis(target))

    @pl.loop(0, NV)
    def _(k):
        d_out[k] = total[pl.ds(pl.multiple_of(k * ROWS, ROWS), ROWS), :].astype(BF16)

    @pl.loop(1, NV)
    def _(d):
        d_copy(j, lax.rem(j + d, NV)).start()

    acc = total[pl.ds(pl.multiple_of(j * ROWS, ROWS), ROWS), :]
    dirty[...] = acc

    @pl.loop(1, NV)
    def _(d):
        k = lax.rem(j + d, NV)
        d_copy(k, k).wait_recv()
        dirty[...] += d_in[k].astype(F32)

    dirty[...] = dirty[...] * F32(1.0 / (S * S))

    @pl.loop(0, NF - 1)
    def _(i):
        h = far_first(i)
        uv_copy(f, h).wait_send()
        p_copy(f, h).wait_send()
        r_copy(f, h).wait_send()

    @pl.loop(1, NV)
    def _(d):
        k = lax.rem(j + d, NV)
        ag_copy(j, k).wait_send()
        d_copy(j, k).wait_send()


def body(model, observed, u_offsets, v_offsets, facet_lists):
    vm = pl.BlockSpec(memory_space=pltpu.VMEM)
    sm = pl.BlockSpec(memory_space=pltpu.SMEM)
    dma = pltpu.SemaphoreType.DMA
    return tuple(
        pl.pallas_call(
            kernel,
            name="major_cycle",
            out_shape=(
                jax.ShapeDtypeStruct((ROWS, FW), F32),
                jax.ShapeDtypeStruct((G, 2, S, S), BF16),
            ),
            in_specs=[vm, vm, sm, sm, sm],
            out_specs=(vm, vm),
            scratch_shapes=[
                pltpu.VMEM((FRT, FW), BF16),
                pltpu.VMEM((NF, 8, LANES), jnp.int32),
                pltpu.VMEM((NF, 8, LANES), jnp.int32),
                pltpu.VMEM((YC, S, LANES), F32),
                pltpu.VMEM((YC, S, LANES), F32),
                pltpu.VMEM((XC, S, LANES), F32),
                pltpu.VMEM((XC, S, LANES), F32),
                pltpu.VMEM((2 * NF, YC, LANES), F32),
                pltpu.VMEM((2 * NF, YC, LANES), F32),
                pltpu.VMEM((2 * NF, 8, LANES), F32),
                pltpu.VMEM((2 * NF, 8, LANES), F32),
                pltpu.VMEM((2 * NF, 2 * S, FW), BF16),
                pltpu.VMEM((2 * NF, 2 * S, FRT), BF16),
                pltpu.VMEM((2 * NF, FRT, 2 * S), BF16),
                pltpu.VMEM((NF, 2, 2, S, S), BF16),
                pltpu.VMEM((2 * NF, 2, S, S), BF16),
                pltpu.VMEM((2 * NF, 2, S, S), BF16),
                pltpu.VMEM((2 * NF, 2, S, S), BF16),
                pltpu.VMEM((FRT, FW), F32),
                pltpu.VMEM((NV, ROWS, FW), BF16),
                pltpu.VMEM((NV, ROWS, FW), BF16),
                dma((NV,)), dma((NV,)), dma((NF,)), dma((NF,)), dma((NF,)), dma((NF,)),
                dma((NF,)), dma((NF,)), dma((NV,)), dma((NV,)),
            ],
            compiler_params=pltpu.CompilerParams(
                collective_id=0, has_side_effects=True, vmem_limit_bytes=56 << 20
            ),
        )(model, observed, u_offsets, v_offsets, facet_lists)
    )


def solution(mesh):
    in_specs = (
        P(("facet", "vis"), None),
        P(("facet", "vis"), None, None, None),
        P(("facet", "vis")),
        P(("facet", "vis")),
        P(("facet", "vis"), None),
    )
    out_specs = (P(("facet", "vis"), None), P(("facet", "vis"), None, None, None))
    return jax.shard_map(body, mesh=mesh, in_specs=in_specs, out_specs=out_specs, check_vma=False)
```

```python
import math

import jax
import jax.numpy as jnp
from jax import lax
from jax.experimental import pallas as pl
from jax.experimental.pallas import tpu as pltpu
from jax.sharding import PartitionSpec as P

IMG = 32768
LANES = 128
NF = 8
NV = 16
S = 128
FW = 2048
FRT = 256
ROWS = 16
G = 8
YC = FW // LANES
XC = FRT // LANES
STEP = IMG // NF
MESH = pl.DeviceIdType.MESH
F32 = jnp.float32
BF16 = jnp.bfloat16
NT = (((1,), (1,)), ((), ()))
NN = (((1,), (0,)), ((), ()))


def sincos(index):
    quarter = (index + IMG // 8) >> 13
    rest = index - (quarter << 13)
    angle = rest.astype(F32) * F32(2.0 * math.pi / IMG)
    t = angle * angle
    sn = angle * (1.0 + t * (-1.0 / 6 + t * (1.0 / 120 + t * (-1.0 / 5040 + t * (1.0 / 362880)))))
    cs = 1.0 + t * (-0.5 + t * (1.0 / 24 + t * (-1.0 / 720 + t * (1.0 / 40320))))
    odd = (quarter & 1) == 1
    c = jnp.where(odd, sn, cs)
    s = jnp.where(odd, cs, sn)
    c = jnp.where(((quarter + 1) & 2) != 0, -c, c)
    s = jnp.where((quarter & 2) != 0, -s, s)
    return c, s


def iota(shape, axis):
    return lax.broadcasted_iota(jnp.int32, shape, axis)


def kernel(
    model, observed, u_off, v_off, lists, dirty, residual,
    obs_v, image, uv_out, uv_in, e_c, e_s, g_c, g_s, pv_c, pv_s, pu_c, pu_s, cv, cu, cut,
    p_out, p_in, r_out, r_in, total, d_out, d_in,
    ag_ss, ag_rs, uv_ss, uv_rs, p_ss, p_rs, r_ss, r_rs, d_ss, d_rs, io,
):
    f = lax.axis_index("facet")
    j = lax.axis_index("vis")

    def other_facet(h):
        return {"facet": h, "vis": j}

    def other_vis(k):
        return {"facet": f, "vis": k}

    def rows(k):
        return pl.ds(pl.multiple_of(k * ROWS, ROWS), ROWS)

    load_model = pltpu.make_async_copy(model, image.at[rows(j), :], io.at[0])
    load_observed = pltpu.make_async_copy(observed, obs_v, io.at[1])
    load_model.start()
    load_observed.start()

    flip = lax.rem(f, 2) == 1
    first_at = lax.select(flip, j // 4, lax.rem(j, 4))
    second_at = lax.select(flip, lax.rem(j, 4), j // 4)

    def place(da, db):
        a = lax.rem(first_at + da, 4)
        b = lax.rem(second_at + db, 4)
        return lax.select(flip, a * 4 + b, b * 4 + a)

    barrier = pltpu.get_barrier_semaphore()
    for d in range(1, 4):
        pl.semaphore_signal(barrier, inc=1, device_id=other_vis(place(d, 0)), device_id_type=MESH)
        pl.semaphore_signal(barrier, inc=1, device_id=other_vis(place(0, d)), device_id_type=MESH)
    for d in range(1, NF):
        pl.semaphore_signal(barrier, inc=1, device_id=other_facet(lax.rem(f + d, NF)), device_id_type=MESH)
    pl.semaphore_wait(barrier, 6 + NF - 1)

    def remote(src, dst, ss, rs, device):
        return pltpu.make_async_remote_copy(
            src_ref=src, dst_ref=dst, send_sem=ss, recv_sem=rs, device_id=device, device_id_type=MESH
        )

    def ag_copy(da, ta, tb):
        owner = place(da, 0)
        return remote(
            image.at[rows(owner), :], image.at[rows(owner), :],
            ag_ss.at[da, ta + tb], ag_rs.at[owner], other_vis(place(ta, tb)),
        )

    def ag_wait(da, db):
        owner = place(da, db)
        remote(
            image.at[rows(owner), :], image.at[rows(owner), :],
            ag_ss.at[0, 0], ag_rs.at[owner], other_vis(owner),
        ).wait_recv()

    def ag_own(d):
        return remote(
            image.at[rows(j), :], image.at[rows(j), :], ag_ss.at[0, 3 + d], ag_rs.at[j], other_vis(place(d, 0))
        )

    load_model.wait()
    for d in (2, 1, 3):
        ag_own(d).start()
    for d in (2, 1, 3):
        ag_copy(0, 0, d).start()

    first, last = [], []
    hits = [[lists[k, g] for k in range(2)] for g in range(G)]
    for h in range(NF):
        lo, hi = jnp.int32(0), jnp.int32(0)
        for g in range(G):
            named = (hits[g][0] == h) | (hits[g][1] == h)
            hi = jnp.where(named, g, hi)
        for g in reversed(range(G)):
            named = (hits[g][0] == h) | (hits[g][1] == h)
            lo = jnp.where(named, g, lo)
        first.append(lo)
        last.append(hi)

    row = iota((8, LANES), 0)
    for h in range(NF):
        a, b = first[h], last[h]
        uv_out[h] = jnp.where(
            row == 0, u_off[a], jnp.where(row == 1, u_off[b], jnp.where(row == 2, v_off[a], v_off[b]))
        )

    def uv_copy(sender, target):
        return remote(uv_out.at[target], uv_in.at[sender], uv_ss.at[target], uv_rs.at[sender], other_facet(target))

    def far_first(i):
        q = i // 2
        dz = jnp.where(q == 0, 2, jnp.where(q == 1, 1, jnp.where(q == 2, 3, 0)))
        z = lax.rem(f // 2 + dz, 4)
        c = lax.rem(lax.rem(f, 2) + 1 + lax.rem(i, 2), 2)
        return z * 2 + c

    @pl.loop(0, NF - 1)
    def _(i):
        uv_copy(f, far_first(i)).start()

    uv_in[f] = uv_out[f]

    lane = iota((S, LANES), 1)
    sub = iota((S, LANES), 0)

    @pl.loop(0, YC)
    def _(r):
        c, s = sincos((sub * (r * LANES + lane)) & (IMG - 1))
        e_c[r] = c
        e_s[r] = s

    @pl.loop(0, XC)
    def _(r):
        c, s = sincos((sub * (f * STEP + r * LANES + lane)) & (IMG - 1))
        g_c[r] = c
        g_s[r] = s

    for da in (1, 3, 2):
        ag_wait(da, 0)
        for d in (2, 1, 3):
            ag_copy(da, 0, d).start()

    @pl.loop(0, NF - 1)
    def _(i):
        uv_copy(far_first(i), far_first(i)).wait_recv()

    y_of = iota((YC, LANES), 0) * LANES + iota((YC, LANES), 1)
    x_of = iota((8, LANES), 0) * LANES + iota((8, LANES), 1) + f * STEP

    @pl.loop(0, NF)
    def _(h):
        for s in range(2):
            u = uv_in[h, s : s + 1, :]
            v = uv_in[h, 2 + s : 3 + s, :]
            c, sn = sincos((v * y_of) & (IMG - 1))
            pv_c[2 * h + s] = c
            pv_s[2 * h + s] = sn
            c, sn = sincos((u * x_of) & (IMG - 1))
            pu_c[2 * h + s] = c
            pu_s[2 * h + s] = sn

    @pl.loop(0, 2 * NF)
    def _(n):
        h = n // 2
        base = lax.rem(n, 2) * (2 * S)
        cos_rows = pl.ds(pl.multiple_of(base, S), S)
        sin_rows = pl.ds(pl.multiple_of(base + S, S), S)

        @pl.loop(0, YC)
        def _(r):
            pc = pv_c[n, pl.ds(r, 1), :]
            ps = pv_s[n, pl.ds(r, 1), :]
            ec, es = e_c[r], e_s[r]
            at = pl.ds(pl.multiple_of(r * LANES, LANES), LANES)
            cv[h, cos_rows, at] = (pc * ec - ps * es).astype(BF16)
            cv[h, sin_rows, at] = (ps * ec + pc * es).astype(BF16)

        for r in range(XC):
            pc = pu_c[n, r : r + 1, :]
            ps = pu_s[n, r : r + 1, :]
            ec, es = g_c[r], g_s[r]
            at = slice(r * LANES, (r + 1) * LANES)
            c = pc * ec - ps * es
            s = ps * ec + pc * es
            cu[n, 0:S, at] = c.astype(BF16)
            cu[n, S : 2 * S, at] = s.astype(BF16)
            cut[n, at, 0:S] = c.T.astype(BF16)
            cut[n, at, S : 2 * S] = s.T.astype(BF16)

    for db in range(1, 4):
        for da in range(4):
            ag_wait(da, db)

    def predict(h):
        t = lax.dot_general(cv[h], image[...], NT, preferred_element_type=F32).astype(BF16)
        for s in range(2):
            o = lax.dot_general(
                cu[2 * h + s], t[2 * S * s : 2 * S * (s + 1)], NT, preferred_element_type=F32
            )
            yield s, (o[0:S, 0:S] - o[S:, S:]).astype(BF16), (-(o[S:, 0:S] + o[0:S, S:])).astype(BF16)

    def p_copy(sender, target):
        return remote(
            p_out.at[target], p_in.at[pl.ds(2 * sender, 2)], p_ss.at[target], p_rs.at[sender], other_facet(target)
        )

    @pl.loop(0, NF)
    def _(i):
        h = far_first(i)
        for s, re, im in predict(h):
            p_out[h, s, 0] = re
            p_out[h, s, 1] = im

        @pl.when(i < NF - 1)
        def _():
            p_copy(f, h).start()

    for s in range(2):
        p_in[2 * f + s] = p_out[f, s]

    @pl.loop(0, NF - 1)
    def _(i):
        p_copy(far_first(i), far_first(i)).wait_recv()

    load_observed.wait()

    for g in range(G):
        acc = obs_v[g].astype(F32)
        for k in range(2):
            h = hits[g][k]
            slot = jnp.int32(0)
            for e in range(g):
                slot = jnp.where((hits[e][0] == h) | (hits[e][1] == h), 1, slot)
            acc = acc - p_in[2 * h + slot].astype(F32)
        residual[g] = acc.astype(BF16)

    def r_copy(sender, target):
        return remote(
            r_out.at[pl.ds(2 * target, 2)], r_in.at[pl.ds(2 * sender, 2)],
            r_ss.at[target], r_rs.at[sender], other_facet(target),
        )

    for h in range(NF):
        r_out[2 * h] = residual[first[h]]
        r_out[2 * h + 1] = residual[last[h]]

    @pl.loop(0, NF - 1)
    def _(i):
        r_copy(f, far_first(i)).start()

    for s in range(2):
        r_in[2 * f + s] = r_out[2 * f + s]

    total[...] = jnp.zeros_like(total)

    @pl.loop(0, NF)
    def _(i):
        h = far_first(lax.select(i < 2, NF - 1 - i, i - 2))

        @pl.when(i > 0)
        def _():
            r_copy(h, h).wait_recv()

        z = []
        for s in range(2):
            re = r_in[2 * h + s, 0]
            im = r_in[2 * h + s, 1]
            top = jnp.concatenate([re, -im], axis=1)
            bottom = jnp.concatenate([-im, -re], axis=1)
            both = jnp.concatenate([top, bottom], axis=0)
            z.append(lax.dot_general(cut[2 * h + s], both, NN, preferred_element_type=F32).astype(BF16))
        total[...] += lax.dot_general(jnp.concatenate(z, axis=1), cv[h], NN, preferred_element_type=F32)

    def d_copy(da, db):
        return remote(
            d_out.at[db, da], d_in.at[4 - db, da], d_ss.at[db, da], d_rs.at[4 - db, da], other_vis(place(0, db))
        )

    def s_copy(da):
        return remote(
            d_out.at[0, da], d_in.at[0, 4 - da], d_ss.at[0, da], d_rs.at[0, 4 - da], other_vis(place(da, 0))
        )

    for da in (2, 1, 3, 0):
        for db in (2, 1, 3):
            d_out[db, da] = total[rows(place(da, db)), :].astype(BF16)
            d_copy(da, db).start()

    def gathered(da):
        acc = total[rows(place(da, 0)), :]
        for db in range(1, 4):
            d_copy(da, 4 - db).wait_recv()
            acc = acc + d_in[db, da].astype(F32)
        return acc

    for da in (2, 1, 3):
        d_out[0, da] = gathered(da).astype(BF16)
        s_copy(da).start()

    acc = gathered(0)
    for da in (2, 1, 3):
        s_copy(4 - da).wait_recv()
        acc = acc + d_in[0, da].astype(F32)
    dirty[...] = acc * F32(1.0 / (S * S))

    @pl.loop(0, NF - 1)
    def _(i):
        h = far_first(i)
        uv_copy(f, h).wait_send()
        p_copy(f, h).wait_send()
        r_copy(f, h).wait_send()

    for d in range(1, 4):
        ag_own(d).wait_send()
        s_copy(d).wait_send()
        for da in range(4):
            ag_copy(da, 0, d).wait_send()
            d_copy(da, d).wait_send()


def body(model, observed, u_offsets, v_offsets, facet_lists):
    hbm = pl.BlockSpec(memory_space=pl.ANY)
    vm = pl.BlockSpec(memory_space=pltpu.VMEM)
    sm = pl.BlockSpec(memory_space=pltpu.SMEM)
    dma = pltpu.SemaphoreType.DMA
    return tuple(pl.pallas_call(
            kernel,
            name="major_cycle",
            out_shape=(pltpu.VMEM((ROWS, FW), F32), pltpu.VMEM((G, 2, S, S), BF16)),
            in_specs=[hbm, hbm, sm, sm, sm],
            out_specs=(vm, vm),
            scratch_shapes=[
                pltpu.VMEM((G, 2, S, S), BF16),
                pltpu.VMEM((FRT, FW), BF16),
                pltpu.VMEM((NF, 8, LANES), jnp.int32),
                pltpu.VMEM((NF, 8, LANES), jnp.int32),
                pltpu.VMEM((YC, S, LANES), F32),
                pltpu.VMEM((YC, S, LANES), F32),
                pltpu.VMEM((XC, S, LANES), F32),
                pltpu.VMEM((XC, S, LANES), F32),
                pltpu.VMEM((2 * NF, YC, LANES), F32),
                pltpu.VMEM((2 * NF, YC, LANES), F32),
                pltpu.VMEM((2 * NF, 8, LANES), F32),
                pltpu.VMEM((2 * NF, 8, LANES), F32),
                pltpu.VMEM((NF, 4 * S, FW), BF16),
                pltpu.VMEM((2 * NF, 2 * S, FRT), BF16),
                pltpu.VMEM((2 * NF, FRT, 2 * S), BF16),
                pltpu.VMEM((NF, 2, 2, S, S), BF16),
                pltpu.VMEM((2 * NF, 2, S, S), BF16),
                pltpu.VMEM((2 * NF, 2, S, S), BF16),
                pltpu.VMEM((2 * NF, 2, S, S), BF16),
                pltpu.VMEM((FRT, FW), F32),
                pltpu.VMEM((4, 4, ROWS, FW), BF16),
                pltpu.VMEM((4, 4, ROWS, FW), BF16),
                dma((4, 8)), dma((NV,)), dma((NF,)), dma((NF,)), dma((NF,)), dma((NF,)),
                dma((NF,)), dma((NF,)), dma((4, 4)), dma((4, 4)), dma((2,)),
            ],
            compiler_params=pltpu.CompilerParams(
                collective_id=0, has_side_effects=True, vmem_limit_bytes=56 << 20
            ),
        )(model, observed, u_offsets, v_offsets, facet_lists.T))


def solution(mesh):
    in_specs = (
        P(("facet", "vis"), None),
        P(("facet", "vis"), None, None, None),
        P(("facet", "vis")),
        P(("facet", "vis")),
        P(("facet", "vis"), None),
    )
    out_specs = (P(("facet", "vis"), None), P(("facet", "vis"), None, None, None))
    return jax.shard_map(body, mesh=mesh, in_specs=in_specs, out_specs=out_specs, check_vma=False)
```

```python
import math

import jax
import jax.numpy as jnp
from jax import lax
from jax.experimental import pallas as pl
from jax.experimental.pallas import tpu as pltpu
from jax.sharding import PartitionSpec as P

IMG = 32768
LANES = 128
NF = 8
NV = 16
S = 128
FW = 2048
FRT = 256
ROWS = 16
G = 8
YC = FW // LANES
XC = FRT // LANES
STEP = IMG // NF
MESH = pl.DeviceIdType.MESH
F32 = jnp.float32
BF16 = jnp.bfloat16
NT = (((1,), (1,)), ((), ()))
NN = (((1,), (0,)), ((), ()))


def sincos(index):
    quarter = (index + IMG // 8) >> 13
    rest = index - (quarter << 13)
    angle = rest.astype(F32) * F32(2.0 * math.pi / IMG)
    t = angle * angle
    sn = angle * (1.0 + t * (-1.0 / 6 + t * (1.0 / 120 + t * (-1.0 / 5040 + t * (1.0 / 362880)))))
    cs = 1.0 + t * (-0.5 + t * (1.0 / 24 + t * (-1.0 / 720 + t * (1.0 / 40320))))
    odd = (quarter & 1) == 1
    c = jnp.where(odd, sn, cs)
    s = jnp.where(odd, cs, sn)
    c = jnp.where(((quarter + 1) & 2) != 0, -c, c)
    s = jnp.where((quarter & 2) != 0, -s, s)
    return c, s


def iota(shape, axis):
    return lax.broadcasted_iota(jnp.int32, shape, axis)


def kernel(
    model, observed, u_hbm, v_hbm, lists_hbm, dirty, residual,
    u_off, v_off, lists, obs_v, image, uv_out, uv_in, e_c, e_s, g_c, g_s, pv_c, pv_s, pu_c, pu_s, cv, cu, cut,
    p_out, p_in, r_out, r_in, total, d_out, d_in,
    ag_ss, ag_rs, uv_ss, uv_rs, p_ss, p_rs, r_ss, r_rs, d_ss, d_rs, hop_ss, hop_rs, up_ss, up_rs, io,
):
    f = lax.axis_index("facet")
    j = lax.axis_index("vis")
    z = f // 2
    c = lax.rem(f, 2)
    far = lax.rem(f + NF // 2, NF)

    def rows(k, which=0):
        return pl.ds(pl.multiple_of(which * FRT + k * ROWS, ROWS), ROWS)

    def remote(src, dst, ss, rs, device):
        return pltpu.make_async_remote_copy(
            src_ref=src, dst_ref=dst, send_sem=ss, recv_sem=rs, device_id=device, device_id_type=MESH
        )

    def other_facet(h):
        return {"facet": h, "vis": j}

    def other_vis(k):
        return {"facet": f, "vis": k}

    def along(q, last_dz):
        return jnp.where(q == 0, 1, jnp.where(q == 1, 3, jnp.where(q == 2, 0, last_dz)))

    def facet_of(p):
        return lax.rem(z + along(p // 2, 2), 4) * 2 + lax.rem(c + lax.rem(p, 2), 2)

    def home_of(p):
        return lax.rem(z + along(p // 2, 0), 4) * 2 + lax.rem(c + lax.rem(p, 2), 2)

    def back(p):
        return jnp.where(p < 2, p + 2, jnp.where(p < 4, p - 2, p))

    def z_first(i):
        return jnp.where(i < 4, 2 * lax.rem(i, 2) + i // 2, i + 1 - 2 * lax.rem(i, 2))

    def two_first(i):
        return jnp.where(i == 0, 2, jnp.where(i == 1, 1, jnp.where(i == 2, 3, 0)))

    load_model = pltpu.make_async_copy(model, image.at[rows(j), :], io.at[0])
    load_observed = pltpu.make_async_copy(observed, obs_v, io.at[1])
    load_small = [
        pltpu.make_async_copy(src, dst, io.at[2 + i])
        for i, (src, dst) in enumerate(((u_hbm, u_off), (v_hbm, v_off), (lists_hbm, lists)))
    ]
    load_model.start()
    for load in load_small:
        load.start()
    load_observed.start()

    flip = c == 1
    first_at = lax.select(flip, j // 4, lax.rem(j, 4))
    second_at = lax.select(flip, lax.rem(j, 4), j // 4)

    def place(da, db):
        a = lax.rem(first_at + da, 4)
        b = lax.rem(second_at + db, 4)
        return lax.select(flip, a * 4 + b, b * 4 + a)

    barrier = pltpu.get_barrier_semaphore()
    for d in range(1, 4):
        pl.semaphore_signal(barrier, inc=1, device_id=other_vis(place(d, 0)), device_id_type=MESH)
        pl.semaphore_signal(barrier, inc=1, device_id=other_vis(place(0, d)), device_id_type=MESH)
    for p in (0, 1, 2, 3, 5):
        pl.semaphore_signal(barrier, inc=1, device_id=other_facet(home_of(p)), device_id_type=MESH)
    pl.semaphore_signal(barrier, inc=1, device_id=other_facet(far), device_id_type=MESH)
    pl.semaphore_wait(barrier, 12)

    def ag_copy(w, da, ta, tb):
        block = image.at[rows(place(da, 0), w), :]
        return remote(
            block, block, ag_ss.at[w, da, ta + 4 * tb], ag_rs.at[w, da, 0 if tb == 0 else 4 - tb]
            if ta == 0 else ag_rs.at[w, 4 - ta, 0], other_vis(place(ta, tb)),
        )

    def ag_wait(w, da, db):
        block = image.at[rows(place(da, db), w), :]
        remote(block, block, ag_ss.at[w, 0, 0], ag_rs.at[w, da, db], other_vis(place(1, 0))).wait_recv()

    def ag_second(w, da):
        for d in (2, 1, 3):
            ag_copy(w, da, 0, d).start()

    def ag_rest(w):
        for db in range(1, 4):
            for da in range(4):
                ag_wait(w, da, db)

    def model_hop(da):
        at = place(da, 0)
        return remote(
            image.at[rows(at), :], image.at[rows(at, 1), :], hop_ss.at[da], hop_rs.at[da], other_facet(far)
        )

    load_model.wait()
    for d in (2, 1, 3):
        ag_copy(0, 0, d, 0).start()
    ag_second(0, 0)
    model_hop(0).start()

    for load in load_small:
        load.wait()

    def listed(h):
        lo, hi = jnp.int32(0), jnp.int32(0)
        for g in range(G):
            hi = jnp.where((lists[0, g] == h) | (lists[1, g] == h), g, hi)
        for g in reversed(range(G)):
            lo = jnp.where((lists[0, g] == h) | (lists[1, g] == h), g, lo)
        return lo, hi

    row = iota((8, LANES), 0)

    @pl.loop(0, 6)
    def _(p):
        tile = jnp.zeros((8, LANES), jnp.int32)
        for half in range(2):
            lo, hi = listed(facet_of(jnp.minimum(p + 2 * half, NF - 1)))
            for at, value in enumerate((u_off[lo], u_off[hi], v_off[lo], v_off[hi])):
                tile = jnp.where(row == 4 * half + at, value, tile)
        uv_out[p] = tile

    def uv_copy(p):
        return remote(uv_out.at[p], uv_in.at[back(p)], uv_ss.at[p], uv_rs.at[back(p)], other_facet(home_of(p)))

    for p in (0, 1, 2, 3, 5):
        uv_copy(p).start()
    uv_in[4] = uv_out[4]

    lane = iota((S, LANES), 1)
    sub = iota((S, LANES), 0)

    @pl.loop(0, XC)
    def _(r):
        for w, facet in enumerate((f, far)):
            co, si = sincos((sub * (facet * STEP + r * LANES + lane)) & (IMG - 1))
            g_c[w, r] = co
            g_s[w, r] = si

    @pl.loop(0, YC)
    def _(r):
        co, si = sincos((sub * (r * LANES + lane)) & (IMG - 1))
        e_c[r] = co
        e_s[r] = si

    for da in (1, 3, 2):
        ag_wait(0, da, 0)
        ag_second(0, da)
        model_hop(da).start()

    for p in (0, 1, 2, 3, 5):
        uv_copy(back(p)).wait_recv()

    y_of = iota((YC, LANES), 0) * LANES + iota((YC, LANES), 1)
    x_of = iota((8, LANES), 0) * LANES + iota((8, LANES), 1)

    @pl.loop(0, 2 * NF)
    def _(n):
        p = n // 2
        w = p // 6
        at = 4 * w + lax.rem(n, 2)
        u = uv_in[p - 2 * w, pl.ds(at, 1), :]
        v = uv_in[p - 2 * w, pl.ds(at + 2, 1), :]
        co, si = sincos((v * y_of) & (IMG - 1))
        pv_c[n] = co
        pv_s[n] = si
        co, si = sincos((u * (x_of + jnp.where(w == 1, far, f) * STEP)) & (IMG - 1))
        pu_c[n] = co
        pu_s[n] = si

    @pl.loop(0, 2 * NF)
    def _(n):
        p = n // 2
        w = p // 6
        base = lax.rem(n, 2) * (2 * S)
        cos_rows = pl.ds(pl.multiple_of(base, S), S)
        sin_rows = pl.ds(pl.multiple_of(base + S, S), S)

        @pl.loop(0, YC)
        def _(r):
            pc = pv_c[n, pl.ds(r, 1), :]
            ps = pv_s[n, pl.ds(r, 1), :]
            ec, es = e_c[r], e_s[r]
            at = pl.ds(pl.multiple_of(r * LANES, LANES), LANES)
            cv[p, cos_rows, at] = (pc * ec - ps * es).astype(BF16)
            cv[p, sin_rows, at] = (ps * ec + pc * es).astype(BF16)

        @pl.loop(0, XC)
        def _(r):
            pc = pu_c[n, pl.ds(r, 1), :]
            ps = pu_s[n, pl.ds(r, 1), :]
            ec, es = g_c[w, r], g_s[w, r]
            at = pl.ds(pl.multiple_of(r * LANES, LANES), LANES)
            co = pc * ec - ps * es
            si = ps * ec + pc * es
            cu[n, 0:S, at] = co.astype(BF16)
            cu[n, S : 2 * S, at] = si.astype(BF16)
            cut[n, at, 0:S] = co.T.astype(BF16)
            cut[n, at, S : 2 * S] = si.T.astype(BF16)

    total[...] = jnp.zeros_like(total)
    ag_rest(0)

    def p_copy(p, s):
        return remote(
            p_out.at[2 * p + s], p_in.at[2 * back(p) + s],
            p_ss.at[2 * p + s], p_rs.at[2 * back(p) + s], other_facet(home_of(p)),
        )

    @pl.loop(0, NF)
    def _(i):
        p = z_first(i)

        @pl.when(i == 1)
        def _():
            for da in (0, 1, 3, 2):
                model_hop(da).wait_recv()
                ag_second(1, da)

        @pl.when(i == 6)
        def _():
            ag_rest(1)

        window = pl.ds(pl.multiple_of(p // 6 * FRT, FRT), FRT)
        t = lax.dot_general(cv[p], image[window, :], NT, preferred_element_type=F32).astype(BF16)
        for s in range(2):
            o = lax.dot_general(
                cu[2 * p + s], t[2 * S * s : 2 * S * (s + 1)], NT, preferred_element_type=F32
            )
            p_out[2 * p + s, 0] = (o[0:S, 0:S] - o[S:, S:]).astype(BF16)
            p_out[2 * p + s, 1] = (-(o[S:, 0:S] + o[0:S, S:])).astype(BF16)

            @pl.when((i != 5) & (i != 7))
            def _():
                p_copy(p, s).start()

    for n in (8, 9, 12, 13):
        p_in[n] = p_out[n]

    load_observed.wait()
    for p in (0, 1, 2, 3, 5, 7):
        for s in range(2):
            p_copy(back(p), s).wait_recv()

    @pl.loop(0, G)
    def _(g):
        acc = obs_v[g].astype(F32)
        for k in range(2):
            h = lists[k, g]
            slot = jnp.int32(0)
            for e in range(G):
                slot = jnp.where((e < g) & ((lists[0, e] == h) | (lists[1, e] == h)), 1, slot)
            dz = (h // 2 - z) & 3
            q = jnp.where(dz == 0, 2, jnp.where(dz == 1, 0, jnp.where(dz == 2, 3, 1)))
            acc = acc - p_in[4 * q + 2 * ((h - c) & 1) + slot].astype(F32)
        residual[g] = acc.astype(BF16)

    def r_copy(p):
        return remote(
            r_out.at[pl.ds(2 * p, 2)], r_in.at[pl.ds(2 * back(p), 2)],
            r_ss.at[p], r_rs.at[back(p)], other_facet(home_of(p)),
        )

    @pl.loop(0, NF)
    def _(i):
        p = z_first(i)
        lo, hi = listed(facet_of(p))
        r_out[2 * p] = residual[lo]
        r_out[2 * p + 1] = residual[hi]

        @pl.when((i < 2) | (i == 4) | (i == 6))
        def _():
            r_copy(p).start()

    for n in (8, 9, 12, 13):
        r_in[n] = r_out[n]

    def d_copy(w, da, db):
        return remote(
            d_out.at[w, db, da], d_in.at[w, 4 - db, da], d_ss.at[w, db, da], d_rs.at[w, 4 - db, da],
            other_vis(place(0, db)),
        )

    def s_copy(da):
        return remote(
            d_out.at[0, 0, da], d_in.at[0, 0, 4 - da], d_ss.at[0, 0, da], d_rs.at[0, 0, 4 - da],
            other_vis(place(da, 0)),
        )

    def image_hop(da):
        return remote(d_out.at[1, 0, da], d_in.at[1, 0, da], up_ss.at[da], up_rs.at[da], other_facet(far))

    def spread(w):
        @pl.loop(0, 12)
        def _(i):
            da = two_first(i // 3)
            db = two_first(lax.rem(i, 3))
            d_out[w, db, da] = total[w, rows(place(da, db)), :].astype(BF16)
            d_copy(w, da, db).start()

    def gathered(w, da):
        acc = total[w, rows(place(da, 0)), :]
        for db in range(1, 4):
            d_copy(w, da, 4 - db).wait_recv()
            acc = acc + d_in[w, db, da].astype(F32)
        return acc

    def both_chips(da):
        acc = gathered(0, da)
        image_hop(da).wait_recv()
        return acc + d_in[1, 0, da].astype(F32)

    @pl.loop(0, NF)
    def _(i):
        p = jnp.where(i < 2, i + 6, jnp.where(i < 4, i + 2, z_first(i - 4)))
        w = jnp.where(i < 2, 1, 0)

        @pl.when(i == 1)
        def _():
            for unit in (1, 3):
                r_copy(unit).start()

        @pl.when(i == 2)
        def _():
            spread(1)

        @pl.when((i != 0) & (i != 2))
        def _():
            r_copy(back(p)).wait_recv()

        zs = []
        for s in range(2):
            re = r_in[2 * p + s, 0]
            im = r_in[2 * p + s, 1]
            top = jnp.concatenate([re, -im], axis=1)
            bottom = jnp.concatenate([-im, -re], axis=1)
            both = jnp.concatenate([top, bottom], axis=0)
            zs.append(lax.dot_general(cut[2 * p + s], both, NN, preferred_element_type=F32).astype(BF16))
        total[w] += lax.dot_general(jnp.concatenate(zs, axis=1), cv[p], NN, preferred_element_type=F32)

    spread(0)

    @pl.loop(0, 4)
    def _(i):
        da = two_first(i)
        d_out[1, 0, da] = gathered(1, da).astype(BF16)
        image_hop(da).start()

    @pl.loop(0, 3)
    def _(i):
        da = two_first(i)
        d_out[0, 0, da] = both_chips(da).astype(BF16)
        s_copy(da).start()

    acc = both_chips(0)
    for da in (2, 1, 3):
        s_copy(4 - da).wait_recv()
        acc = acc + d_in[0, 0, da].astype(F32)
    dirty[...] = acc * F32(1.0 / (S * S))

    for p in (0, 1, 2, 3, 5):
        uv_copy(p).wait_send()
    for p in (0, 1, 2, 3, 5, 7):
        r_copy(p).wait_send()
        for s in range(2):
            p_copy(p, s).wait_send()
    for da in range(4):
        model_hop(da).wait_send()
        image_hop(da).wait_send()
        for d in range(1, 4):
            for w in range(2):
                ag_copy(w, da, 0, d).wait_send()
                d_copy(w, da, d).wait_send()
    for d in range(1, 4):
        ag_copy(0, 0, d, 0).wait_send()
        s_copy(d).wait_send()


def body(model, observed, u_offsets, v_offsets, facet_lists):
    hbm = pl.BlockSpec(memory_space=pl.ANY)
    vm = pl.BlockSpec(memory_space=pltpu.VMEM)
    dma = pltpu.SemaphoreType.DMA
    return tuple(pl.pallas_call(
            kernel,
            name="major_cycle",
            out_shape=(pltpu.VMEM((ROWS, FW), F32), pltpu.VMEM((G, 2, S, S), BF16)),
            in_specs=[hbm] * 5,
            out_specs=(vm, vm),
            scratch_shapes=[
                pltpu.SMEM((G,), jnp.int32),
                pltpu.SMEM((G,), jnp.int32),
                pltpu.SMEM((2, G), jnp.int32),
                pltpu.VMEM((G, 2, S, S), BF16),
                pltpu.VMEM((2 * FRT, FW), BF16),
                pltpu.VMEM((6, 8, LANES), jnp.int32),
                pltpu.VMEM((6, 8, LANES), jnp.int32),
                pltpu.VMEM((YC, S, LANES), F32),
                pltpu.VMEM((YC, S, LANES), F32),
                pltpu.VMEM((2, XC, S, LANES), F32),
                pltpu.VMEM((2, XC, S, LANES), F32),
                pltpu.VMEM((2 * NF, YC, LANES), F32),
                pltpu.VMEM((2 * NF, YC, LANES), F32),
                pltpu.VMEM((2 * NF, 8, LANES), F32),
                pltpu.VMEM((2 * NF, 8, LANES), F32),
                pltpu.VMEM((NF, 4 * S, FW), BF16),
                pltpu.VMEM((2 * NF, 2 * S, FRT), BF16),
                pltpu.VMEM((2 * NF, FRT, 2 * S), BF16),
                pltpu.VMEM((2 * NF, 2, S, S), BF16),
                pltpu.VMEM((2 * NF, 2, S, S), BF16),
                pltpu.VMEM((2 * NF, 2, S, S), BF16),
                pltpu.VMEM((2 * NF, 2, S, S), BF16),
                pltpu.VMEM((2, FRT, FW), F32),
                pltpu.VMEM((2, 4, 4, ROWS, FW), BF16),
                pltpu.VMEM((2, 4, 4, ROWS, FW), BF16),
                dma((2, 4, 16)), dma((2, 4, 4)), dma((6,)), dma((6,)), dma((2 * NF,)), dma((2 * NF,)),
                dma((NF,)), dma((NF,)), dma((2, 4, 4)), dma((2, 4, 4)),
                dma((4,)), dma((4,)), dma((4,)), dma((4,)), dma((5,)),
            ],
            compiler_params=pltpu.CompilerParams(
                collective_id=0, has_side_effects=True, vmem_limit_bytes=56 << 20
            ),
        )(model, observed, u_offsets, v_offsets, facet_lists.T))


def solution(mesh):
    in_specs = (
        P(("facet", "vis"), None),
        P(("facet", "vis"), None, None, None),
        P(("facet", "vis")),
        P(("facet", "vis")),
        P(("facet", "vis"), None),
    )
    out_specs = (P(("facet", "vis"), None), P(("facet", "vis"), None, None, None))
    return jax.shard_map(body, mesh=mesh, in_specs=in_specs, out_specs=out_specs, check_vma=False)
```

```python
import math

import jax
import jax.numpy as jnp
from jax import lax
from jax.experimental import pallas as pl
from jax.experimental.pallas import tpu as pltpu
from jax.sharding import PartitionSpec as P

IMG = 32768
LANES = 128
NF = 8
NV = 16
S = 128
FW = 2048
FRT = 256
ROWS = 16
G = 8
YC = FW // LANES
XC = FRT // LANES
STEP = IMG // NF
MESH = pl.DeviceIdType.MESH
F32 = jnp.float32
BF16 = jnp.bfloat16
NT = (((1,), (1,)), ((), ()))
NN = (((1,), (0,)), ((), ()))


def sincos(index):
    quarter = (index + IMG // 8) >> 13
    rest = index - (quarter << 13)
    angle = rest.astype(F32) * F32(2.0 * math.pi / IMG)
    t = angle * angle
    sn = angle * (1.0 + t * (-1.0 / 6 + t * (1.0 / 120 + t * (-1.0 / 5040 + t * (1.0 / 362880)))))
    cs = 1.0 + t * (-0.5 + t * (1.0 / 24 + t * (-1.0 / 720 + t * (1.0 / 40320))))
    odd = (quarter & 1) == 1
    c = jnp.where(odd, sn, cs)
    s = jnp.where(odd, cs, sn)
    c = jnp.where(((quarter + 1) & 2) != 0, -c, c)
    s = jnp.where((quarter & 2) != 0, -s, s)
    return c, s


def iota(shape, axis):
    return lax.broadcasted_iota(jnp.int32, shape, axis)


def kernel(
    model, observed, u_hbm, v_hbm, lists_hbm, dirty, residual,
    u_off, v_off, lists, obs_v, image, uv_out, uv_in, e_c, e_s, g_c, g_s, pv_c, pv_s, pu_c, pu_s, cv, cu, cut,
    p_out, p_in, r_out, r_in, total, d_out, d_in,
    ag_ss, ag_rs, uv_ss, uv_rs, p_ss, p_rs, r_ss, r_rs, d_ss, d_rs, hop_ss, hop_rs, up_ss, up_rs, io,
):
    f = lax.axis_index("facet")
    j = lax.axis_index("vis")
    z = f // 2
    c = lax.rem(f, 2)
    far = lax.rem(f + NF // 2, NF)

    def rows(k, which=0):
        return pl.ds(pl.multiple_of(which * FRT + k * ROWS, ROWS), ROWS)

    def remote(src, dst, ss, rs, device):
        return pltpu.make_async_remote_copy(
            src_ref=src, dst_ref=dst, send_sem=ss, recv_sem=rs, device_id=device, device_id_type=MESH
        )

    def other_facet(h):
        return {"facet": h, "vis": j}

    def other_vis(k):
        return {"facet": f, "vis": k}

    def along(q, last_dz):
        return jnp.where(q == 0, 1, jnp.where(q == 1, 3, jnp.where(q == 2, 0, last_dz)))

    def facet_of(p):
        return lax.rem(z + along(p // 2, 2), 4) * 2 + lax.rem(c + lax.rem(p, 2), 2)

    def home_of(p):
        return lax.rem(z + along(p // 2, 0), 4) * 2 + lax.rem(c + lax.rem(p, 2), 2)

    def back(p):
        return jnp.where(p < 2, p + 2, jnp.where(p < 4, p - 2, p))

    def z_first(i):
        return jnp.where(i < 4, 2 * lax.rem(i, 2) + i // 2, i + 1 - 2 * lax.rem(i, 2))

    def two_first(i):
        return jnp.where(i == 0, 2, jnp.where(i == 1, 1, jnp.where(i == 2, 3, 0)))

    load_model = pltpu.make_async_copy(model, image.at[rows(j), :], io.at[0])
    load_observed = pltpu.make_async_copy(observed, obs_v, io.at[1])
    load_small = [
        pltpu.make_async_copy(src, dst, io.at[2 + i])
        for i, (src, dst) in enumerate(((u_hbm, u_off), (v_hbm, v_off), (lists_hbm, lists)))
    ]
    load_model.start()
    for load in load_small:
        load.start()
    load_observed.start()

    flip = c == 1
    first_at = lax.select(flip, j // 4, lax.rem(j, 4))
    second_at = lax.select(flip, lax.rem(j, 4), j // 4)

    def place(da, db):
        a = lax.rem(first_at + da, 4)
        b = lax.rem(second_at + db, 4)
        return lax.select(flip, a * 4 + b, b * 4 + a)

    barrier = pltpu.get_barrier_semaphore()
    for d in range(1, 4):
        pl.semaphore_signal(barrier, inc=1, device_id=other_vis(place(d, 0)), device_id_type=MESH)
        pl.semaphore_signal(barrier, inc=1, device_id=other_vis(place(0, d)), device_id_type=MESH)
    for p in (0, 1, 2, 3, 5):
        pl.semaphore_signal(barrier, inc=1, device_id=other_facet(home_of(p)), device_id_type=MESH)
    pl.semaphore_signal(barrier, inc=1, device_id=other_facet(far), device_id_type=MESH)
    pl.semaphore_wait(barrier, 12)

    def ag_copy(w, da, ta, tb):
        block = image.at[rows(place(da, 0), w), :]
        return remote(
            block, block, ag_ss.at[w, da, ta + 4 * tb], ag_rs.at[w, da, 0 if tb == 0 else 4 - tb]
            if ta == 0 else ag_rs.at[w, 4 - ta, 0], other_vis(place(ta, tb)),
        )

    def ag_wait(w, da, db):
        block = image.at[rows(place(da, db), w), :]
        remote(block, block, ag_ss.at[w, 0, 0], ag_rs.at[w, da, db], other_vis(place(1, 0))).wait_recv()

    def ag_second(w, da):
        for d in (2, 1, 3):
            ag_copy(w, da, 0, d).start()

    def ag_rest(w):
        for db in range(1, 4):
            for da in range(4):
                ag_wait(w, da, db)

    def model_hop(da):
        at = place(da, 0)
        return remote(
            image.at[rows(at), :], image.at[rows(at, 1), :], hop_ss.at[da], hop_rs.at[da], other_facet(far)
        )

    load_model.wait()
    for d in (2, 1, 3):
        ag_copy(0, 0, d, 0).start()
    ag_second(0, 0)
    model_hop(0).start()

    for load in load_small:
        load.wait()

    def listed(h):
        lo, hi = jnp.int32(0), jnp.int32(0)
        for g in range(G):
            hi = jnp.where((lists[0, g] == h) | (lists[1, g] == h), g, hi)
        for g in reversed(range(G)):
            lo = jnp.where((lists[0, g] == h) | (lists[1, g] == h), g, lo)
        return lo, hi

    row = iota((8, LANES), 0)

    @pl.loop(0, 6)
    def _(p):
        tile = jnp.zeros((8, LANES), jnp.int32)
        for half in range(2):
            lo, hi = listed(facet_of(jnp.minimum(p + 2 * half, NF - 1)))
            for at, value in enumerate((u_off[lo], u_off[hi], v_off[lo], v_off[hi])):
                tile = jnp.where(row == 4 * half + at, value, tile)
        uv_out[p] = tile

    def uv_copy(p):
        return remote(uv_out.at[p], uv_in.at[back(p)], uv_ss.at[p], uv_rs.at[back(p)], other_facet(home_of(p)))

    for p in (0, 1, 2, 3, 5):
        uv_copy(p).start()
    uv_in[4] = uv_out[4]

    lane = iota((S, LANES), 1)
    sub = iota((S, LANES), 0)

    @pl.loop(0, XC)
    def _(r):
        for w, facet in enumerate((f, far)):
            co, si = sincos((sub * (facet * STEP + r * LANES + lane)) & (IMG - 1))
            g_c[w, r] = co
            g_s[w, r] = si

    @pl.loop(0, YC)
    def _(r):
        co, si = sincos((sub * (r * LANES + lane)) & (IMG - 1))
        e_c[r] = co
        e_s[r] = si

    for da in (1, 3, 2):
        ag_wait(0, da, 0)
        ag_second(0, da)
        model_hop(da).start()

    for p in (0, 1, 2, 3, 5):
        uv_copy(back(p)).wait_recv()

    y_of = iota((YC, LANES), 0) * LANES + iota((YC, LANES), 1)
    x_of = iota((8, LANES), 0) * LANES + iota((8, LANES), 1)

    @pl.loop(0, 2 * NF)
    def _(n):
        p = n // 2
        w = p // 6
        at = 4 * w + lax.rem(n, 2)
        u = uv_in[p - 2 * w, pl.ds(at, 1), :]
        v = uv_in[p - 2 * w, pl.ds(at + 2, 1), :]
        co, si = sincos((v * y_of) & (IMG - 1))
        pv_c[n] = co
        pv_s[n] = si
        co, si = sincos((u * (x_of + jnp.where(w == 1, far, f) * STEP)) & (IMG - 1))
        pu_c[n] = co
        pu_s[n] = si

    total[...] = jnp.zeros_like(total)

    def p_copy(p, s):
        return remote(
            p_out.at[2 * p + s], p_in.at[2 * back(p) + s],
            p_ss.at[2 * p + s], p_rs.at[2 * back(p) + s], other_facet(home_of(p)),
        )

    @pl.loop(0, 2)
    def _(half):
        @pl.loop(NF * half, NF * half + NF)
        def _(n):
            p = n // 2
            w = p // 6
            base = lax.rem(n, 2) * (2 * S)
            cos_rows = pl.ds(pl.multiple_of(base, S), S)
            sin_rows = pl.ds(pl.multiple_of(base + S, S), S)

            @pl.loop(0, YC, step=16)
            def _(r0):
                for k in range(16):
                    r = r0 + k
                    pc = pv_c[n, pl.ds(r, 1), :]
                    ps = pv_s[n, pl.ds(r, 1), :]
                    ec, es = e_c[r], e_s[r]
                    at = pl.ds(pl.multiple_of(r * LANES, LANES), LANES)
                    cv[p, cos_rows, at] = (pc * ec - ps * es).astype(BF16)
                    cv[p, sin_rows, at] = (ps * ec + pc * es).astype(BF16)

            @pl.loop(0, XC)
            def _(r):
                pc = pu_c[n, pl.ds(r, 1), :]
                ps = pu_s[n, pl.ds(r, 1), :]
                ec, es = g_c[w, r], g_s[w, r]
                at = pl.ds(pl.multiple_of(r * LANES, LANES), LANES)
                co = pc * ec - ps * es
                si = ps * ec + pc * es
                cu[n, 0:S, at] = co.astype(BF16)
                cu[n, S : 2 * S, at] = si.astype(BF16)

        @pl.when(half == 0)
        def _():
            ag_rest(0)

        @pl.loop(4 * half, 4 * half + 4)
        def _(i):
            p = z_first(i)

            @pl.when(i == 1)
            def _():
                for da in (0, 1, 3, 2):
                    model_hop(da).wait_recv()
                    ag_second(1, da)

            @pl.when(i == 6)
            def _():
                ag_rest(1)

            window = pl.ds(pl.multiple_of(p // 6 * FRT, FRT), FRT)
            t = lax.dot_general(cv[p], image[window, :], NT, preferred_element_type=F32).astype(BF16)
            for s in range(2):
                o = lax.dot_general(
                    cu[2 * p + s], t[2 * S * s : 2 * S * (s + 1)], NT, preferred_element_type=F32
                )
                p_out[2 * p + s, 0] = (o[0:S, 0:S] - o[S:, S:]).astype(BF16)
                p_out[2 * p + s, 1] = (-(o[S:, 0:S] + o[0:S, S:])).astype(BF16)

                @pl.when((i != 5) & (i != 7))
                def _():
                    p_copy(p, s).start()

    @pl.loop(0, 2 * NF)
    def _(n):
        for r in range(XC):
            at = slice(r * LANES, (r + 1) * LANES)
            for k in range(2):
                cut[n, at, k * S : (k + 1) * S] = cu[n, k * S : (k + 1) * S, at].T

    for n in (8, 9, 12, 13):
        p_in[n] = p_out[n]

    load_observed.wait()
    for p in (0, 1, 2, 3, 5, 7):
        for s in range(2):
            p_copy(back(p), s).wait_recv()

    @pl.loop(0, G)
    def _(g):
        acc = obs_v[g].astype(F32)
        for k in range(2):
            h = lists[k, g]
            slot = jnp.int32(0)
            for e in range(G):
                slot = jnp.where((e < g) & ((lists[0, e] == h) | (lists[1, e] == h)), 1, slot)
            dz = (h // 2 - z) & 3
            q = jnp.where(dz == 0, 2, jnp.where(dz == 1, 0, jnp.where(dz == 2, 3, 1)))
            acc = acc - p_in[4 * q + 2 * ((h - c) & 1) + slot].astype(F32)
        residual[g] = acc.astype(BF16)

    def r_copy(p):
        return remote(
            r_out.at[pl.ds(2 * p, 2)], r_in.at[pl.ds(2 * back(p), 2)],
            r_ss.at[p], r_rs.at[back(p)], other_facet(home_of(p)),
        )

    @pl.loop(0, NF)
    def _(i):
        p = z_first(i)
        lo, hi = listed(facet_of(p))
        r_out[2 * p] = residual[lo]
        r_out[2 * p + 1] = residual[hi]

        @pl.when((i < 2) | (i == 4) | (i == 6))
        def _():
            r_copy(p).start()

    for n in (8, 9, 12, 13):
        r_in[n] = r_out[n]

    def d_copy(w, da, db):
        return remote(
            d_out.at[w, db, da], d_in.at[w, 4 - db, da], d_ss.at[w, db, da], d_rs.at[w, 4 - db, da],
            other_vis(place(0, db)),
        )

    def s_copy(da):
        return remote(
            d_out.at[0, 0, da], d_in.at[0, 0, 4 - da], d_ss.at[0, 0, da], d_rs.at[0, 0, 4 - da],
            other_vis(place(da, 0)),
        )

    def image_hop(da):
        return remote(d_out.at[1, 0, da], d_in.at[1, 0, da], up_ss.at[da], up_rs.at[da], other_facet(far))

    def spread(w):
        @pl.loop(0, 12)
        def _(i):
            da = two_first(i // 3)
            db = two_first(lax.rem(i, 3))
            d_out[w, db, da] = total[w, rows(place(da, db)), :].astype(BF16)
            d_copy(w, da, db).start()

    def gathered(w, da):
        acc = total[w, rows(place(da, 0)), :]
        for db in range(1, 4):
            d_copy(w, da, 4 - db).wait_recv()
            acc = acc + d_in[w, db, da].astype(F32)
        return acc

    def both_chips(da):
        acc = gathered(0, da)
        image_hop(da).wait_recv()
        return acc + d_in[1, 0, da].astype(F32)

    @pl.loop(0, NF)
    def _(i):
        p = jnp.where(i < 2, i + 6, jnp.where(i < 4, i + 2, z_first(i - 4)))
        w = jnp.where(i < 2, 1, 0)

        @pl.when(i == 1)
        def _():
            for unit in (1, 3):
                r_copy(unit).start()

        @pl.when(i == 2)
        def _():
            spread(1)

        @pl.when((i != 0) & (i != 2))
        def _():
            r_copy(back(p)).wait_recv()

        zs = []
        for s in range(2):
            re = r_in[2 * p + s, 0]
            im = r_in[2 * p + s, 1]
            top = jnp.concatenate([re, -im], axis=1)
            bottom = jnp.concatenate([-im, -re], axis=1)
            both = jnp.concatenate([top, bottom], axis=0)
            zs.append(lax.dot_general(cut[2 * p + s], both, NN, preferred_element_type=F32).astype(BF16))
        total[w] += lax.dot_general(jnp.concatenate(zs, axis=1), cv[p], NN, preferred_element_type=F32)

    spread(0)

    @pl.loop(0, 4)
    def _(i):
        da = two_first(i)
        d_out[1, 0, da] = gathered(1, da).astype(BF16)
        image_hop(da).start()

    @pl.loop(0, 3)
    def _(i):
        da = two_first(i)
        d_out[0, 0, da] = both_chips(da).astype(BF16)
        s_copy(da).start()

    acc = both_chips(0)
    for da in (2, 1, 3):
        s_copy(4 - da).wait_recv()
        acc = acc + d_in[0, 0, da].astype(F32)
    dirty[...] = acc * F32(1.0 / (S * S))

    for p in (0, 1, 2, 3, 5):
        uv_copy(p).wait_send()
    for p in (0, 1, 2, 3, 5, 7):
        r_copy(p).wait_send()
        for s in range(2):
            p_copy(p, s).wait_send()
    for da in range(4):
        model_hop(da).wait_send()
        image_hop(da).wait_send()
        for d in range(1, 4):
            for w in range(2):
                ag_copy(w, da, 0, d).wait_send()
                d_copy(w, da, d).wait_send()
    for d in range(1, 4):
        ag_copy(0, 0, d, 0).wait_send()
        s_copy(d).wait_send()


def body(model, observed, u_offsets, v_offsets, facet_lists):
    hbm = pl.BlockSpec(memory_space=pl.ANY)
    vm = pl.BlockSpec(memory_space=pltpu.VMEM)
    dma = pltpu.SemaphoreType.DMA
    return tuple(pl.pallas_call(
            kernel,
            name="major_cycle",
            out_shape=(pltpu.VMEM((ROWS, FW), F32), pltpu.VMEM((G, 2, S, S), BF16)),
            in_specs=[hbm] * 5,
            out_specs=(vm, vm),
            scratch_shapes=[
                pltpu.SMEM((G,), jnp.int32),
                pltpu.SMEM((G,), jnp.int32),
                pltpu.SMEM((2, G), jnp.int32),
                pltpu.VMEM((G, 2, S, S), BF16),
                pltpu.VMEM((2 * FRT, FW), BF16),
                pltpu.VMEM((6, 8, LANES), jnp.int32),
                pltpu.VMEM((6, 8, LANES), jnp.int32),
                pltpu.VMEM((YC, S, LANES), F32),
                pltpu.VMEM((YC, S, LANES), F32),
                pltpu.VMEM((2, XC, S, LANES), F32),
                pltpu.VMEM((2, XC, S, LANES), F32),
                pltpu.VMEM((2 * NF, YC, LANES), F32),
                pltpu.VMEM((2 * NF, YC, LANES), F32),
                pltpu.VMEM((2 * NF, 8, LANES), F32),
                pltpu.VMEM((2 * NF, 8, LANES), F32),
                pltpu.VMEM((NF, 4 * S, FW), BF16),
                pltpu.VMEM((2 * NF, 2 * S, FRT), BF16),
                pltpu.VMEM((2 * NF, FRT, 2 * S), BF16),
                pltpu.VMEM((2 * NF, 2, S, S), BF16),
                pltpu.VMEM((2 * NF, 2, S, S), BF16),
                pltpu.VMEM((2 * NF, 2, S, S), BF16),
                pltpu.VMEM((2 * NF, 2, S, S), BF16),
                pltpu.VMEM((2, FRT, FW), F32),
                pltpu.VMEM((2, 4, 4, ROWS, FW), BF16),
                pltpu.VMEM((2, 4, 4, ROWS, FW), BF16),
                dma((2, 4, 16)), dma((2, 4, 4)), dma((6,)), dma((6,)), dma((2 * NF,)), dma((2 * NF,)),
                dma((NF,)), dma((NF,)), dma((2, 4, 4)), dma((2, 4, 4)),
                dma((4,)), dma((4,)), dma((4,)), dma((4,)), dma((5,)),
            ],
            compiler_params=pltpu.CompilerParams(
                collective_id=0, has_side_effects=True, vmem_limit_bytes=56 << 20
            ),
        )(model, observed, u_offsets, v_offsets, facet_lists.T))


def solution(mesh):
    in_specs = (
        P(("facet", "vis"), None),
        P(("facet", "vis"), None, None, None),
        P(("facet", "vis")),
        P(("facet", "vis")),
        P(("facet", "vis"), None),
    )
    out_specs = (P(("facet", "vis"), None), P(("facet", "vis"), None, None, None))
    return jax.shard_map(body, mesh=mesh, in_specs=in_specs, out_specs=out_specs, check_vma=False)
```

```python
import math

import jax
import jax.numpy as jnp
from jax import lax
from jax.experimental import pallas as pl
from jax.experimental.pallas import tpu as pltpu
from jax.sharding import PartitionSpec as P

IMG = 32768
LANES = 128
NF = 8
NV = 16
S = 128
FW = 2048
FRT = 256
ROWS = 16
G = 8
YC = FW // LANES
XC = FRT // LANES
STEP = IMG // NF
MESH = pl.DeviceIdType.MESH
F32 = jnp.float32
BF16 = jnp.bfloat16
NT = (((1,), (1,)), ((), ()))
NN = (((1,), (0,)), ((), ()))


def sincos(index):
    quarter = (index + IMG // 8) >> 13
    rest = index - (quarter << 13)
    angle = rest.astype(F32) * F32(2.0 * math.pi / IMG)
    t = angle * angle
    sn = angle * (1.0 + t * (-1.0 / 6 + t * (1.0 / 120 + t * (-1.0 / 5040 + t * (1.0 / 362880)))))
    cs = 1.0 + t * (-0.5 + t * (1.0 / 24 + t * (-1.0 / 720 + t * (1.0 / 40320))))
    odd = (quarter & 1) == 1
    c = jnp.where(odd, sn, cs)
    s = jnp.where(odd, cs, sn)
    c = jnp.where(((quarter + 1) & 2) != 0, -c, c)
    s = jnp.where((quarter & 2) != 0, -s, s)
    return c, s


def iota(shape, axis):
    return lax.broadcasted_iota(jnp.int32, shape, axis)


def kernel(
    model, observed, u_hbm, v_hbm, lists_hbm, dirty, residual,
    u_off, v_off, lists, obs_v, image, uv_out, uv_in, e_c, e_s, g_c, g_s, pv_c, pv_s, pu_c, pu_s, cv_a, cv_b, cu_a, cu_b, cut,
    p_out, p_in, r_out, r_in, total, d_out, d_in,
    ag_ss, ag_rs, uv_ss, uv_rs, p_ss, p_rs, r_ss, r_rs, d_ss, d_rs, hop_ss, hop_rs, up_ss, up_rs, io,
):
    f = lax.axis_index("facet")
    j = lax.axis_index("vis")
    z = f // 2
    c = lax.rem(f, 2)
    far = lax.rem(f + NF // 2, NF)

    def rows(k, which=0):
        return pl.ds(pl.multiple_of(which * FRT + k * ROWS, ROWS), ROWS)

    def remote(src, dst, ss, rs, device):
        return pltpu.make_async_remote_copy(
            src_ref=src, dst_ref=dst, send_sem=ss, recv_sem=rs, device_id=device, device_id_type=MESH
        )

    def other_facet(h):
        return {"facet": h, "vis": j}

    def other_vis(k):
        return {"facet": f, "vis": k}

    def along(q, last_dz):
        return jnp.where(q == 0, 1, jnp.where(q == 1, 3, jnp.where(q == 2, 0, last_dz)))

    def facet_of(p):
        return lax.rem(z + along(p // 2, 2), 4) * 2 + lax.rem(c + lax.rem(p, 2), 2)

    def home_of(p):
        return lax.rem(z + along(p // 2, 0), 4) * 2 + lax.rem(c + lax.rem(p, 2), 2)

    def back(p):
        return jnp.where(p < 2, p + 2, jnp.where(p < 4, p - 2, p))

    def z_first(i):
        return jnp.where(i < 4, 2 * lax.rem(i, 2) + i // 2, i + 1 - 2 * lax.rem(i, 2))

    def two_first(i):
        return jnp.where(i == 0, 2, jnp.where(i == 1, 1, jnp.where(i == 2, 3, 0)))

    load_model = pltpu.make_async_copy(model, image.at[rows(j), :], io.at[0])
    load_observed = pltpu.make_async_copy(observed, obs_v, io.at[1])
    load_small = [
        pltpu.make_async_copy(src, dst, io.at[2 + i])
        for i, (src, dst) in enumerate(((u_hbm, u_off), (v_hbm, v_off), (lists_hbm, lists)))
    ]
    load_model.start()
    for load in load_small:
        load.start()
    load_observed.start()

    flip = c == 1
    first_at = lax.select(flip, j // 4, lax.rem(j, 4))
    second_at = lax.select(flip, lax.rem(j, 4), j // 4)

    def place(da, db):
        a = lax.rem(first_at + da, 4)
        b = lax.rem(second_at + db, 4)
        return lax.select(flip, a * 4 + b, b * 4 + a)

    barrier = pltpu.get_barrier_semaphore()
    for d in range(1, 4):
        pl.semaphore_signal(barrier, inc=1, device_id=other_vis(place(d, 0)), device_id_type=MESH)
        pl.semaphore_signal(barrier, inc=1, device_id=other_vis(place(0, d)), device_id_type=MESH)
    for p in (0, 1, 2, 3, 5):
        pl.semaphore_signal(barrier, inc=1, device_id=other_facet(home_of(p)), device_id_type=MESH)
    pl.semaphore_signal(barrier, inc=1, device_id=other_facet(far), device_id_type=MESH)
    pl.semaphore_wait(barrier, 12)

    def ag_copy(w, da, ta, tb):
        block = image.at[rows(place(da, 0), w), :]
        return remote(
            block, block, ag_ss.at[w, da, ta + 4 * tb], ag_rs.at[w, da, 0 if tb == 0 else 4 - tb]
            if ta == 0 else ag_rs.at[w, 4 - ta, 0], other_vis(place(ta, tb)),
        )

    def ag_wait(w, da, db):
        block = image.at[rows(place(da, db), w), :]
        remote(block, block, ag_ss.at[w, 0, 0], ag_rs.at[w, da, db], other_vis(place(1, 0))).wait_recv()

    def ag_second(w, da):
        for d in (2, 1, 3):
            ag_copy(w, da, 0, d).start()

    def ag_rest(w):
        for db in range(1, 4):
            for da in range(4):
                ag_wait(w, da, db)

    def model_hop(da):
        at = place(da, 0)
        return remote(
            image.at[rows(at), :], image.at[rows(at, 1), :], hop_ss.at[da], hop_rs.at[da], other_facet(far)
        )

    load_model.wait()
    for d in (2, 1, 3):
        ag_copy(0, 0, d, 0).start()
    ag_second(0, 0)
    model_hop(0).start()

    for load in load_small:
        load.wait()

    def listed(h):
        lo, hi = jnp.int32(0), jnp.int32(0)
        for g in range(G):
            hi = jnp.where((lists[0, g] == h) | (lists[1, g] == h), g, hi)
        for g in reversed(range(G)):
            lo = jnp.where((lists[0, g] == h) | (lists[1, g] == h), g, lo)
        return lo, hi

    row = iota((8, LANES), 0)

    @pl.loop(0, 6)
    def _(p):
        tile = jnp.zeros((8, LANES), jnp.int32)
        for half in range(2):
            lo, hi = listed(facet_of(jnp.minimum(p + 2 * half, NF - 1)))
            for at, value in enumerate((u_off[lo], u_off[hi], v_off[lo], v_off[hi])):
                tile = jnp.where(row == 4 * half + at, value, tile)
        uv_out[p] = tile

    def uv_copy(p):
        return remote(uv_out.at[p], uv_in.at[back(p)], uv_ss.at[p], uv_rs.at[back(p)], other_facet(home_of(p)))

    for p in (0, 1, 2, 3, 5):
        uv_copy(p).start()
    uv_in[4] = uv_out[4]

    lane = iota((S, LANES), 1)
    sub = iota((S, LANES), 0)

    @pl.loop(0, XC)
    def _(r):
        for w, facet in enumerate((f, far)):
            co, si = sincos((sub * (facet * STEP + r * LANES + lane)) & (IMG - 1))
            g_c[w, r] = co
            g_s[w, r] = si

    @pl.loop(0, YC)
    def _(r):
        co, si = sincos((sub * (r * LANES + lane)) & (IMG - 1))
        e_c[r] = co
        e_s[r] = si

    for da in (1, 3, 2):
        ag_wait(0, da, 0)
        ag_second(0, da)
        model_hop(da).start()

    for p in (0, 1, 2, 3, 5):
        uv_copy(back(p)).wait_recv()

    y_of = iota((YC, LANES), 0) * LANES + iota((YC, LANES), 1)
    x_of = iota((8, LANES), 0) * LANES + iota((8, LANES), 1)

    @pl.loop(0, 2 * NF)
    def _(n):
        p = n // 2
        w = p // 6
        at = 4 * w + lax.rem(n, 2)
        u = uv_in[p - 2 * w, pl.ds(at, 1), :]
        v = uv_in[p - 2 * w, pl.ds(at + 2, 1), :]
        co, si = sincos((v * y_of) & (IMG - 1))
        pv_c[n] = co
        pv_s[n] = si
        co, si = sincos((u * (x_of + jnp.where(w == 1, far, f) * STEP)) & (IMG - 1))
        pu_c[n] = co
        pu_s[n] = si

    total[...] = jnp.zeros_like(total)

    def p_copy(p, s):
        return remote(
            p_out.at[2 * p + s], p_in.at[2 * back(p) + s],
            p_ss.at[2 * p + s], p_rs.at[2 * back(p) + s], other_facet(home_of(p)),
        )

    def tables(p, s, cv, cu, k):
        n = 2 * p + s
        w = p // 6
        base = 2 * S * s
        for r in range(YC):
            pc = pv_c[n, r : r + 1, :]
            ps = pv_s[n, r : r + 1, :]
            ec, es = e_c[r], e_s[r]
            at = slice(r * LANES, (r + 1) * LANES)
            cv[k, base : base + S, at] = (pc * ec - ps * es).astype(BF16)
            cv[k, base + S : base + 2 * S, at] = (ps * ec + pc * es).astype(BF16)
        for r in range(XC):
            pc = pu_c[n, r : r + 1, :]
            ps = pu_s[n, r : r + 1, :]
            ec, es = g_c[w, r], g_s[w, r]
            at = slice(r * LANES, (r + 1) * LANES)
            cu[2 * k + s, 0:S, at] = (pc * ec - ps * es).astype(BF16)
            cu[2 * k + s, S : 2 * S, at] = (ps * ec + pc * es).astype(BF16)

    def predict(p, window, cv, cu, k):
        t = lax.dot_general(cv[k], image[window, :], NT, preferred_element_type=F32).astype(BF16)
        for s in range(2):
            o = lax.dot_general(
                cu[2 * k + s], t[2 * S * s : 2 * S * (s + 1)], NT, preferred_element_type=F32
            )
            p_out[2 * p + s, 0] = (o[0:S, 0:S] - o[S:, S:]).astype(BF16)
            p_out[2 * p + s, 1] = (-(o[S:, 0:S] + o[0:S, S:])).astype(BF16)

    @pl.loop(0, 4)
    def _(p):
        for s in range(2):
            tables(p, s, cv_a, cu_a, p)

    @pl.loop(0, 4)
    def _(p):
        for s in range(2):
            tables(p + 4, s, cv_b, cu_b, p)

    ag_rest(0)

    @pl.loop(0, 4)
    def _(i):
        p = z_first(i)

        @pl.when(i == 1)
        def _():
            for da in (0, 1, 3, 2):
                model_hop(da).wait_recv()
                ag_second(1, da)

        predict(p, slice(0, FRT), cv_a, cu_a, p)
        for s in range(2):
            p_copy(p, s).start()

    @pl.loop(4, NF)
    def _(i):
        p = z_first(i)

        @pl.when(i == 6)
        def _():
            ag_rest(1)

        predict(p, pl.ds(pl.multiple_of(p // 6 * FRT, FRT), FRT), cv_b, cu_b, p - 4)

        @pl.when(lax.rem(i, 2) == 0)
        def _():
            for s in range(2):
                p_copy(p, s).start()

    @pl.loop(0, NF)
    def _(n):
        for r in range(XC):
            at = slice(r * LANES, (r + 1) * LANES)
            for k in range(2):
                rest = slice(k * S, (k + 1) * S)
                cut[n, at, rest] = cu_a[n, rest, at].T
                cut[NF + n, at, rest] = cu_b[n, rest, at].T

    for n in (8, 9, 12, 13):
        p_in[n] = p_out[n]

    load_observed.wait()
    for p in (0, 1, 2, 3, 5, 7):
        for s in range(2):
            p_copy(back(p), s).wait_recv()

    @pl.loop(0, G)
    def _(g):
        acc = obs_v[g].astype(F32)
        for k in range(2):
            h = lists[k, g]
            slot = jnp.int32(0)
            for e in range(G):
                slot = jnp.where((e < g) & ((lists[0, e] == h) | (lists[1, e] == h)), 1, slot)
            dz = (h // 2 - z) & 3
            q = jnp.where(dz == 0, 2, jnp.where(dz == 1, 0, jnp.where(dz == 2, 3, 1)))
            acc = acc - p_in[4 * q + 2 * ((h - c) & 1) + slot].astype(F32)
        residual[g] = acc.astype(BF16)

    def r_copy(p):
        return remote(
            r_out.at[pl.ds(2 * p, 2)], r_in.at[pl.ds(2 * back(p), 2)],
            r_ss.at[p], r_rs.at[back(p)], other_facet(home_of(p)),
        )

    @pl.loop(0, NF)
    def _(i):
        p = z_first(i)
        lo, hi = listed(facet_of(p))
        r_out[2 * p] = residual[lo]
        r_out[2 * p + 1] = residual[hi]

        @pl.when((i < 2) | (i == 4) | (i == 6))
        def _():
            r_copy(p).start()

    for n in (8, 9, 12, 13):
        r_in[n] = r_out[n]

    def d_copy(w, da, db):
        return remote(
            d_out.at[w, db, da], d_in.at[w, 4 - db, da], d_ss.at[w, db, da], d_rs.at[w, 4 - db, da],
            other_vis(place(0, db)),
        )

    def s_copy(da):
        return remote(
            d_out.at[0, 0, da], d_in.at[0, 0, 4 - da], d_ss.at[0, 0, da], d_rs.at[0, 0, 4 - da],
            other_vis(place(da, 0)),
        )

    def image_hop(da):
        return remote(d_out.at[1, 0, da], d_in.at[1, 0, da], up_ss.at[da], up_rs.at[da], other_facet(far))

    def spread(w):
        @pl.loop(0, 12)
        def _(i):
            da = two_first(i // 3)
            db = two_first(lax.rem(i, 3))
            d_out[w, db, da] = total[w, rows(place(da, db)), :].astype(BF16)
            d_copy(w, da, db).start()

    def gathered(w, da):
        acc = total[w, rows(place(da, 0)), :]
        for db in range(1, 4):
            d_copy(w, da, 4 - db).wait_recv()
            acc = acc + d_in[w, db, da].astype(F32)
        return acc

    def both_chips(da):
        acc = gathered(0, da)
        image_hop(da).wait_recv()
        return acc + d_in[1, 0, da].astype(F32)

    def grid(p, w, cv, k):
        zs = []
        for s in range(2):
            re = r_in[2 * p + s, 0]
            im = r_in[2 * p + s, 1]
            top = jnp.concatenate([re, -im], axis=1)
            bottom = jnp.concatenate([-im, -re], axis=1)
            both = jnp.concatenate([top, bottom], axis=0)
            zs.append(lax.dot_general(cut[2 * p + s], both, NN, preferred_element_type=F32).astype(BF16))
        total[w] += lax.dot_general(jnp.concatenate(zs, axis=1), cv[k], NN, preferred_element_type=F32)

    @pl.loop(0, 4)
    def _(i):
        p = jnp.where(i < 2, i + 6, i + 2)

        @pl.when(i == 1)
        def _():
            for unit in (1, 3):
                r_copy(unit).start()

        @pl.when(i == 2)
        def _():
            spread(1)

        @pl.when(lax.rem(i, 2) == 1)
        def _():
            r_copy(p).wait_recv()

        grid(p, jnp.where(i < 2, 1, 0), cv_b, p - 4)

    @pl.loop(0, 4)
    def _(i):
        p = z_first(i)
        r_copy(back(p)).wait_recv()
        grid(p, 0, cv_a, p)

    spread(0)

    @pl.loop(0, 4)
    def _(i):
        da = two_first(i)
        d_out[1, 0, da] = gathered(1, da).astype(BF16)
        image_hop(da).start()

    @pl.loop(0, 3)
    def _(i):
        da = two_first(i)
        d_out[0, 0, da] = both_chips(da).astype(BF16)
        s_copy(da).start()

    acc = both_chips(0)
    for da in (2, 1, 3):
        s_copy(4 - da).wait_recv()
        acc = acc + d_in[0, 0, da].astype(F32)
    dirty[...] = acc * F32(1.0 / (S * S))

    for p in (0, 1, 2, 3, 5):
        uv_copy(p).wait_send()
    for p in (0, 1, 2, 3, 5, 7):
        r_copy(p).wait_send()
        for s in range(2):
            p_copy(p, s).wait_send()
    for da in range(4):
        model_hop(da).wait_send()
        image_hop(da).wait_send()
        for d in range(1, 4):
            for w in range(2):
                ag_copy(w, da, 0, d).wait_send()
                d_copy(w, da, d).wait_send()
    for d in range(1, 4):
        ag_copy(0, 0, d, 0).wait_send()
        s_copy(d).wait_send()


def body(model, observed, u_offsets, v_offsets, facet_lists):
    hbm = pl.BlockSpec(memory_space=pl.ANY)
    vm = pl.BlockSpec(memory_space=pltpu.VMEM)
    dma = pltpu.SemaphoreType.DMA
    return tuple(pl.pallas_call(
            kernel,
            name="major_cycle",
            out_shape=(pltpu.VMEM((ROWS, FW), F32), pltpu.VMEM((G, 2, S, S), BF16)),
            in_specs=[hbm] * 5,
            out_specs=(vm, vm),
            scratch_shapes=[
                pltpu.SMEM((G,), jnp.int32),
                pltpu.SMEM((G,), jnp.int32),
                pltpu.SMEM((2, G), jnp.int32),
                pltpu.VMEM((G, 2, S, S), BF16),
                pltpu.VMEM((2 * FRT, FW), BF16),
                pltpu.VMEM((6, 8, LANES), jnp.int32),
                pltpu.VMEM((6, 8, LANES), jnp.int32),
                pltpu.VMEM((YC, S, LANES), F32),
                pltpu.VMEM((YC, S, LANES), F32),
                pltpu.VMEM((2, XC, S, LANES), F32),
                pltpu.VMEM((2, XC, S, LANES), F32),
                pltpu.VMEM((2 * NF, YC, LANES), F32),
                pltpu.VMEM((2 * NF, YC, LANES), F32),
                pltpu.VMEM((2 * NF, 8, LANES), F32),
                pltpu.VMEM((2 * NF, 8, LANES), F32),
                pltpu.VMEM((4, 4 * S, FW), BF16),
                pltpu.VMEM((4, 4 * S, FW), BF16),
                pltpu.VMEM((NF, 2 * S, FRT), BF16),
                pltpu.VMEM((NF, 2 * S, FRT), BF16),
                pltpu.VMEM((2 * NF, FRT, 2 * S), BF16),
                pltpu.VMEM((2 * NF, 2, S, S), BF16),
                pltpu.VMEM((2 * NF, 2, S, S), BF16),
                pltpu.VMEM((2 * NF, 2, S, S), BF16),
                pltpu.VMEM((2 * NF, 2, S, S), BF16),
                pltpu.VMEM((2, FRT, FW), F32),
                pltpu.VMEM((2, 4, 4, ROWS, FW), BF16),
                pltpu.VMEM((2, 4, 4, ROWS, FW), BF16),
                dma((2, 4, 16)), dma((2, 4, 4)), dma((6,)), dma((6,)), dma((2 * NF,)), dma((2 * NF,)),
                dma((NF,)), dma((NF,)), dma((2, 4, 4)), dma((2, 4, 4)),
                dma((4,)), dma((4,)), dma((4,)), dma((4,)), dma((5,)),
            ],
            compiler_params=pltpu.CompilerParams(
                collective_id=0, has_side_effects=True, vmem_limit_bytes=56 << 20
            ),
        )(model, observed, u_offsets, v_offsets, facet_lists.T))


def solution(mesh):
    in_specs = (
        P(("facet", "vis"), None),
        P(("facet", "vis"), None, None, None),
        P(("facet", "vis")),
        P(("facet", "vis")),
        P(("facet", "vis"), None),
    )
    out_specs = (P(("facet", "vis"), None), P(("facet", "vis"), None, None, None))
    return jax.shard_map(body, mesh=mesh, in_specs=in_specs, out_specs=out_specs, check_vma=False)
```

```python
import math

import jax
import jax.numpy as jnp
from jax import lax
from jax.experimental import pallas as pl
from jax.experimental.pallas import tpu as pltpu
from jax.sharding import PartitionSpec as P

IMG = 32768
LANES = 128
NF = 8
NV = 16
S = 128
FW = 2048
FRT = 256
ROWS = 16
G = 8
YC = FW // LANES
XC = FRT // LANES
STEP = IMG // NF
MESH = pl.DeviceIdType.MESH
F32 = jnp.float32
BF16 = jnp.bfloat16
NT = (((1,), (1,)), ((), ()))
NN = (((1,), (0,)), ((), ()))


def sincos(index):
    quarter = (index + IMG // 8) >> 13
    rest = index - (quarter << 13)
    angle = rest.astype(F32) * F32(2.0 * math.pi / IMG)
    t = angle * angle
    sn = angle * (1.0 + t * (-1.0 / 6 + t * (1.0 / 120 + t * (-1.0 / 5040 + t * (1.0 / 362880)))))
    cs = 1.0 + t * (-0.5 + t * (1.0 / 24 + t * (-1.0 / 720 + t * (1.0 / 40320))))
    odd = (quarter & 1) == 1
    c = jnp.where(odd, sn, cs)
    s = jnp.where(odd, cs, sn)
    c = jnp.where(((quarter + 1) & 2) != 0, -c, c)
    s = jnp.where((quarter & 2) != 0, -s, s)
    return c, s


def iota(shape, axis):
    return lax.broadcasted_iota(jnp.int32, shape, axis)


def kernel(
    model, observed, u_hbm, v_hbm, lists_hbm, dirty, residual,
    u_off, v_off, lists, obs_v, image, uv_out, uv_in, e_c, e_s, g_c, g_s, pv_c, pv_s, pu_c, pu_s, cv_a, cv_b, cu_a, cu_b, cut,
    p_out, p_in, r_out, r_in, total, d_out, d_in,
    ag_ss, ag_rs, uv_ss, uv_rs, p_ss, p_rs, r_ss, r_rs, d_ss, d_rs, hop_ss, hop_rs, up_ss, up_rs, io,
):
    f = lax.axis_index("facet")
    j = lax.axis_index("vis")
    z = f // 2
    c = lax.rem(f, 2)
    far = lax.rem(f + NF // 2, NF)

    def rows(k, which=0):
        return pl.ds(pl.multiple_of(which * FRT + k * ROWS, ROWS), ROWS)

    def remote(src, dst, ss, rs, device):
        return pltpu.make_async_remote_copy(
            src_ref=src, dst_ref=dst, send_sem=ss, recv_sem=rs, device_id=device, device_id_type=MESH
        )

    def other_facet(h):
        return {"facet": h, "vis": j}

    def other_vis(k):
        return {"facet": f, "vis": k}

    def along(q, last_dz):
        return jnp.where(q == 0, 1, jnp.where(q == 1, 3, jnp.where(q == 2, 0, last_dz)))

    def facet_of(p):
        return lax.rem(z + along(p // 2, 2), 4) * 2 + lax.rem(c + lax.rem(p, 2), 2)

    def home_of(p):
        return lax.rem(z + along(p // 2, 0), 4) * 2 + lax.rem(c + lax.rem(p, 2), 2)

    def back(p):
        return jnp.where(p < 2, p + 2, jnp.where(p < 4, p - 2, p))

    def z_first(i):
        return jnp.where(i < 4, 2 * lax.rem(i, 2) + i // 2, i + 1 - 2 * lax.rem(i, 2))

    def two_first(i):
        return jnp.where(i == 0, 2, jnp.where(i == 1, 1, jnp.where(i == 2, 3, 0)))

    load_model = pltpu.make_async_copy(model, image.at[rows(j), :], io.at[0])
    load_observed = pltpu.make_async_copy(observed, obs_v, io.at[1])
    load_small = [
        pltpu.make_async_copy(src, dst, io.at[2 + i])
        for i, (src, dst) in enumerate(((u_hbm, u_off), (v_hbm, v_off), (lists_hbm, lists)))
    ]
    load_model.start()
    for load in load_small:
        load.start()
    load_observed.start()

    flip = c == 1
    first_at = lax.select(flip, j // 4, lax.rem(j, 4))
    second_at = lax.select(flip, lax.rem(j, 4), j // 4)

    def place(da, db):
        a = lax.rem(first_at + da, 4)
        b = lax.rem(second_at + db, 4)
        return lax.select(flip, a * 4 + b, b * 4 + a)

    barrier = pltpu.get_barrier_semaphore()
    for d in range(1, 4):
        pl.semaphore_signal(barrier, inc=1, device_id=other_vis(place(d, 0)), device_id_type=MESH)
        pl.semaphore_signal(barrier, inc=1, device_id=other_vis(place(0, d)), device_id_type=MESH)
    for p in (0, 1, 2, 3, 5):
        pl.semaphore_signal(barrier, inc=1, device_id=other_facet(home_of(p)), device_id_type=MESH)
    pl.semaphore_signal(barrier, inc=1, device_id=other_facet(far), device_id_type=MESH)
    pl.semaphore_wait(barrier, 12)

    def ag_copy(w, da, ta, tb):
        block = image.at[rows(place(da, 0), w), :]
        return remote(
            block, block, ag_ss.at[w, da, ta + 4 * tb], ag_rs.at[w, da, 0 if tb == 0 else 4 - tb]
            if ta == 0 else ag_rs.at[w, 4 - ta, 0], other_vis(place(ta, tb)),
        )

    def ag_wait(w, da, db):
        block = image.at[rows(place(da, db), w), :]
        remote(block, block, ag_ss.at[w, 0, 0], ag_rs.at[w, da, db], other_vis(place(1, 0))).wait_recv()

    def ag_second(w, da):
        for d in (2, 1, 3):
            ag_copy(w, da, 0, d).start()

    def ag_rest(w):
        for db in range(1, 4):
            for da in range(4):
                ag_wait(w, da, db)

    def model_hop(da):
        at = place(da, 0)
        return remote(
            image.at[rows(at), :], image.at[rows(at, 1), :], hop_ss.at[da], hop_rs.at[da], other_facet(far)
        )

    load_model.wait()
    for d in (2, 1, 3):
        ag_copy(0, 0, d, 0).start()
    ag_second(0, 0)
    model_hop(0).start()

    for load in load_small:
        load.wait()

    def listed(h):
        lo, hi = jnp.int32(0), jnp.int32(0)
        for g in range(G):
            hi = jnp.where((lists[0, g] == h) | (lists[1, g] == h), g, hi)
        for g in reversed(range(G)):
            lo = jnp.where((lists[0, g] == h) | (lists[1, g] == h), g, lo)
        return lo, hi

    row = iota((8, LANES), 0)

    @pl.loop(0, 6)
    def _(p):
        tile = jnp.zeros((8, LANES), jnp.int32)
        for half in range(2):
            lo, hi = listed(facet_of(jnp.minimum(p + 2 * half, NF - 1)))
            for at, value in enumerate((u_off[lo], u_off[hi], v_off[lo], v_off[hi])):
                tile = jnp.where(row == 4 * half + at, value, tile)
        uv_out[p] = tile

    def uv_copy(p):
        return remote(uv_out.at[p], uv_in.at[back(p)], uv_ss.at[p], uv_rs.at[back(p)], other_facet(home_of(p)))

    for p in (0, 1, 2, 3, 5):
        uv_copy(p).start()
    uv_in[4] = uv_out[4]

    lane = iota((S, LANES), 1)
    sub = iota((S, LANES), 0)

    @pl.loop(0, XC)
    def _(r):
        for w, facet in enumerate((f, far)):
            co, si = sincos((sub * (facet * STEP + r * LANES + lane)) & (IMG - 1))
            g_c[w, r] = co
            g_s[w, r] = si

    @pl.loop(0, YC)
    def _(r):
        co, si = sincos((sub * (r * LANES + lane)) & (IMG - 1))
        e_c[r] = co
        e_s[r] = si

    for da in (1, 3, 2):
        ag_wait(0, da, 0)
        ag_second(0, da)
        model_hop(da).start()

    for p in (0, 1, 2, 3, 5):
        uv_copy(back(p)).wait_recv()

    y_of = iota((YC, LANES), 0) * LANES + iota((YC, LANES), 1)
    x_of = iota((8, LANES), 0) * LANES + iota((8, LANES), 1)

    @pl.loop(0, 2 * NF)
    def _(n):
        p = n // 2
        w = p // 6
        at = 4 * w + lax.rem(n, 2)
        u = uv_in[p - 2 * w, pl.ds(at, 1), :]
        v = uv_in[p - 2 * w, pl.ds(at + 2, 1), :]
        co, si = sincos((v * y_of) & (IMG - 1))
        pv_c[n] = co
        pv_s[n] = si
        co, si = sincos((u * (x_of + jnp.where(w == 1, far, f) * STEP)) & (IMG - 1))
        pu_c[n] = co
        pu_s[n] = si

    total[...] = jnp.zeros_like(total)

    def p_copy(p, s):
        return remote(
            p_out.at[2 * p + s], p_in.at[2 * back(p) + s],
            p_ss.at[2 * p + s], p_rs.at[2 * back(p) + s], other_facet(home_of(p)),
        )

    def tables(p, s, cv, cu, k):
        n = 2 * p + s
        w = p // 6
        base = 2 * S * s
        for r in range(YC):
            pc = pv_c[n, r : r + 1, :]
            ps = pv_s[n, r : r + 1, :]
            ec, es = e_c[r], e_s[r]
            at = slice(r * LANES, (r + 1) * LANES)
            cv[k, base : base + S, at] = (pc * ec - ps * es).astype(BF16)
            cv[k, base + S : base + 2 * S, at] = (ps * ec + pc * es).astype(BF16)
        for r in range(XC):
            pc = pu_c[n, r : r + 1, :]
            ps = pu_s[n, r : r + 1, :]
            ec, es = g_c[w, r], g_s[w, r]
            at = slice(r * LANES, (r + 1) * LANES)
            cu[2 * k + s, 0:S, at] = (pc * ec - ps * es).astype(BF16)
            cu[2 * k + s, S : 2 * S, at] = (ps * ec + pc * es).astype(BF16)

    def predict(p, window, cv, cu, k):
        t = lax.dot_general(cv[k], image[window, :], NT, preferred_element_type=F32).astype(BF16)
        for s in range(2):
            o = lax.dot_general(
                cu[2 * k + s], t[2 * S * s : 2 * S * (s + 1)], NT, preferred_element_type=F32
            )
            p_out[2 * p + s, 0] = (o[0:S, 0:S] - o[S:, S:]).astype(BF16)
            p_out[2 * p + s, 1] = (-(o[S:, 0:S] + o[0:S, S:])).astype(BF16)

    @pl.loop(0, 4)
    def _(p):
        for s in range(2):
            tables(p, s, cv_a, cu_a, p)

    for da in (0, 1, 3, 2):
        model_hop(da).wait_recv()
        ag_second(1, da)

    @pl.loop(0, 4)
    def _(p):
        for s in range(2):
            tables(p + 4, s, cv_b, cu_b, p)

    ag_rest(0)

    @pl.loop(0, 4)
    def _(i):
        p = z_first(i)

        predict(p, slice(0, FRT), cv_a, cu_a, p)
        for s in range(2):
            p_copy(p, s).start()

    @pl.loop(4, NF)
    def _(i):
        p = z_first(i)

        @pl.when(i == 6)
        def _():
            ag_rest(1)

        predict(p, pl.ds(pl.multiple_of(p // 6 * FRT, FRT), FRT), cv_b, cu_b, p - 4)

        @pl.when(lax.rem(i, 2) == 0)
        def _():
            for s in range(2):
                p_copy(p, s).start()

    @pl.loop(0, NF)
    def _(n):
        for r in range(XC):
            at = slice(r * LANES, (r + 1) * LANES)
            for k in range(2):
                rest = slice(k * S, (k + 1) * S)
                cut[n, at, rest] = cu_a[n, rest, at].T
                cut[NF + n, at, rest] = cu_b[n, rest, at].T

    for n in (8, 9, 12, 13):
        p_in[n] = p_out[n]

    load_observed.wait()
    for p in (0, 1, 2, 3, 5, 7):
        for s in range(2):
            p_copy(back(p), s).wait_recv()

    @pl.loop(0, G)
    def _(g):
        acc = obs_v[g].astype(F32)
        for k in range(2):
            h = lists[k, g]
            slot = jnp.int32(0)
            for e in range(G):
                slot = jnp.where((e < g) & ((lists[0, e] == h) | (lists[1, e] == h)), 1, slot)
            dz = (h // 2 - z) & 3
            q = jnp.where(dz == 0, 2, jnp.where(dz == 1, 0, jnp.where(dz == 2, 3, 1)))
            acc = acc - p_in[4 * q + 2 * ((h - c) & 1) + slot].astype(F32)
        residual[g] = acc.astype(BF16)

    def r_copy(p):
        return remote(
            r_out.at[pl.ds(2 * p, 2)], r_in.at[pl.ds(2 * back(p), 2)],
            r_ss.at[p], r_rs.at[back(p)], other_facet(home_of(p)),
        )

    @pl.loop(0, NF)
    def _(i):
        p = z_first(i)
        lo, hi = listed(facet_of(p))
        r_out[2 * p] = residual[lo]
        r_out[2 * p + 1] = residual[hi]

        @pl.when((i < 2) | (i == 4) | (i == 6))
        def _():
            r_copy(p).start()

    for n in (8, 9, 12, 13):
        r_in[n] = r_out[n]

    def d_copy(w, da, db):
        return remote(
            d_out.at[w, db, da], d_in.at[w, 4 - db, da], d_ss.at[w, db, da], d_rs.at[w, 4 - db, da],
            other_vis(place(0, db)),
        )

    def s_copy(da):
        return remote(
            d_out.at[0, 0, da], d_in.at[0, 0, 4 - da], d_ss.at[0, 0, da], d_rs.at[0, 0, 4 - da],
            other_vis(place(da, 0)),
        )

    def image_hop(da):
        return remote(d_out.at[1, 0, da], d_in.at[1, 0, da], up_ss.at[da], up_rs.at[da], other_facet(far))

    def spread(w):
        @pl.loop(0, 12)
        def _(i):
            da = two_first(i // 3)
            db = two_first(lax.rem(i, 3))
            d_out[w, db, da] = total[w, rows(place(da, db)), :].astype(BF16)
            d_copy(w, da, db).start()

    def gathered(w, da):
        acc = total[w, rows(place(da, 0)), :]
        for db in range(1, 4):
            d_copy(w, da, 4 - db).wait_recv()
            acc = acc + d_in[w, db, da].astype(F32)
        return acc

    def both_chips(da):
        acc = gathered(0, da)
        image_hop(da).wait_recv()
        return acc + d_in[1, 0, da].astype(F32)

    def grid(p, w, cv, k):
        zs = []
        for s in range(2):
            re = r_in[2 * p + s, 0]
            im = r_in[2 * p + s, 1]
            top = jnp.concatenate([re, -im], axis=1)
            bottom = jnp.concatenate([-im, -re], axis=1)
            both = jnp.concatenate([top, bottom], axis=0)
            zs.append(lax.dot_general(cut[2 * p + s], both, NN, preferred_element_type=F32).astype(BF16))
        total[w] += lax.dot_general(jnp.concatenate(zs, axis=1), cv[k], NN, preferred_element_type=F32)

    @pl.loop(0, 4)
    def _(i):
        p = jnp.where(i < 2, i + 6, i + 2)

        @pl.when(i == 1)
        def _():
            for unit in (1, 3):
                r_copy(unit).start()

        @pl.when(i == 2)
        def _():
            spread(1)

        @pl.when(lax.rem(i, 2) == 1)
        def _():
            r_copy(p).wait_recv()

        grid(p, jnp.where(i < 2, 1, 0), cv_b, p - 4)

    @pl.loop(0, 4)
    def _(i):
        p = z_first(i)
        r_copy(back(p)).wait_recv()
        grid(p, 0, cv_a, p)

    spread(0)

    @pl.loop(0, 4)
    def _(i):
        da = two_first(i)
        d_out[1, 0, da] = gathered(1, da).astype(BF16)
        image_hop(da).start()

    @pl.loop(0, 3)
    def _(i):
        da = two_first(i)
        d_out[0, 0, da] = both_chips(da).astype(BF16)
        s_copy(da).start()

    acc = both_chips(0)
    for da in (2, 1, 3):
        s_copy(4 - da).wait_recv()
        acc = acc + d_in[0, 0, da].astype(F32)
    dirty[...] = acc * F32(1.0 / (S * S))

    for p in (0, 1, 2, 3, 5):
        uv_copy(p).wait_send()
    for p in (0, 1, 2, 3, 5, 7):
        r_copy(p).wait_send()
        for s in range(2):
            p_copy(p, s).wait_send()
    for da in range(4):
        model_hop(da).wait_send()
        image_hop(da).wait_send()
        for d in range(1, 4):
            for w in range(2):
                ag_copy(w, da, 0, d).wait_send()
                d_copy(w, da, d).wait_send()
    for d in range(1, 4):
        ag_copy(0, 0, d, 0).wait_send()
        s_copy(d).wait_send()


def body(model, observed, u_offsets, v_offsets, facet_lists):
    hbm = pl.BlockSpec(memory_space=pl.ANY)
    vm = pl.BlockSpec(memory_space=pltpu.VMEM)
    dma = pltpu.SemaphoreType.DMA
    return tuple(pl.pallas_call(
            kernel,
            name="major_cycle",
            out_shape=(pltpu.VMEM((ROWS, FW), F32), pltpu.VMEM((G, 2, S, S), BF16)),
            in_specs=[hbm] * 5,
            out_specs=(vm, vm),
            scratch_shapes=[
                pltpu.SMEM((G,), jnp.int32),
                pltpu.SMEM((G,), jnp.int32),
                pltpu.SMEM((2, G), jnp.int32),
                pltpu.VMEM((G, 2, S, S), BF16),
                pltpu.VMEM((2 * FRT, FW), BF16),
                pltpu.VMEM((6, 8, LANES), jnp.int32),
                pltpu.VMEM((6, 8, LANES), jnp.int32),
                pltpu.VMEM((YC, S, LANES), F32),
                pltpu.VMEM((YC, S, LANES), F32),
                pltpu.VMEM((2, XC, S, LANES), F32),
                pltpu.VMEM((2, XC, S, LANES), F32),
                pltpu.VMEM((2 * NF, YC, LANES), F32),
                pltpu.VMEM((2 * NF, YC, LANES), F32),
                pltpu.VMEM((2 * NF, 8, LANES), F32),
                pltpu.VMEM((2 * NF, 8, LANES), F32),
                pltpu.VMEM((4, 4 * S, FW), BF16),
                pltpu.VMEM((4, 4 * S, FW), BF16),
                pltpu.VMEM((NF, 2 * S, FRT), BF16),
                pltpu.VMEM((NF, 2 * S, FRT), BF16),
                pltpu.VMEM((2 * NF, FRT, 2 * S), BF16),
                pltpu.VMEM((2 * NF, 2, S, S), BF16),
                pltpu.VMEM((2 * NF, 2, S, S), BF16),
                pltpu.VMEM((2 * NF, 2, S, S), BF16),
                pltpu.VMEM((2 * NF, 2, S, S), BF16),
                pltpu.VMEM((2, FRT, FW), F32),
                pltpu.VMEM((2, 4, 4, ROWS, FW), BF16),
                pltpu.VMEM((2, 4, 4, ROWS, FW), BF16),
                dma((2, 4, 16)), dma((2, 4, 4)), dma((6,)), dma((6,)), dma((2 * NF,)), dma((2 * NF,)),
                dma((NF,)), dma((NF,)), dma((2, 4, 4)), dma((2, 4, 4)),
                dma((4,)), dma((4,)), dma((4,)), dma((4,)), dma((5,)),
            ],
            compiler_params=pltpu.CompilerParams(
                collective_id=0, has_side_effects=True, vmem_limit_bytes=56 << 20
            ),
        )(model, observed, u_offsets, v_offsets, facet_lists.T))


def solution(mesh):
    in_specs = (
        P(("facet", "vis"), None),
        P(("facet", "vis"), None, None, None),
        P(("facet", "vis")),
        P(("facet", "vis")),
        P(("facet", "vis"), None),
    )
    out_specs = (P(("facet", "vis"), None), P(("facet", "vis"), None, None, None))
    return jax.shard_map(body, mesh=mesh, in_specs=in_specs, out_specs=out_specs, check_vma=False)
```

```python
import math

import jax
import jax.numpy as jnp
from jax import lax
from jax.experimental import pallas as pl
from jax.experimental.pallas import tpu as pltpu
from jax.sharding import PartitionSpec as P

IMG = 32768
LANES = 128
NF = 8
NV = 16
S = 128
FW = 2048
FRT = 256
ROWS = 16
G = 8
YC = FW // LANES
XC = FRT // LANES
STEP = IMG // NF
MESH = pl.DeviceIdType.MESH
F32 = jnp.float32
BF16 = jnp.bfloat16
NT = (((1,), (1,)), ((), ()))
NN = (((1,), (0,)), ((), ()))


def sincos(index):
    quarter = (index + IMG // 8) >> 13
    rest = index - (quarter << 13)
    angle = rest.astype(F32) * F32(2.0 * math.pi / IMG)
    t = angle * angle
    sn = angle * (1.0 + t * (-1.0 / 6 + t * (1.0 / 120 + t * (-1.0 / 5040 + t * (1.0 / 362880)))))
    cs = 1.0 + t * (-0.5 + t * (1.0 / 24 + t * (-1.0 / 720 + t * (1.0 / 40320))))
    odd = (quarter & 1) == 1
    c = jnp.where(odd, sn, cs)
    s = jnp.where(odd, cs, sn)
    c = jnp.where(((quarter + 1) & 2) != 0, -c, c)
    s = jnp.where((quarter & 2) != 0, -s, s)
    return c, s


def iota(shape, axis):
    return lax.broadcasted_iota(jnp.int32, shape, axis)


def kernel(
    model, observed, u_hbm, v_hbm, lists_hbm, dirty, residual,
    u_off, v_off, lists, obs_v, image, uv_out, uv_in, e_c, e_s, g_c, g_s, pv_c, pv_s, pu_c, pu_s, cv_a, cv_b, cu_a, cu_b, cut,
    p_out, p_in, r_out, r_in, total, d_out, d_in,
    ag_ss, ag_rs, uv_ss, uv_rs, p_ss, p_rs, r_ss, r_rs, d_ss, d_rs, hop_ss, hop_rs, up_ss, up_rs, io,
):
    f = lax.axis_index("facet")
    j = lax.axis_index("vis")
    z = f // 2
    c = lax.rem(f, 2)
    far = lax.rem(f + NF // 2, NF)

    def rows(k, which=0):
        return pl.ds(pl.multiple_of(which * FRT + k * ROWS, ROWS), ROWS)

    def remote(src, dst, ss, rs, device):
        return pltpu.make_async_remote_copy(
            src_ref=src, dst_ref=dst, send_sem=ss, recv_sem=rs, device_id=device, device_id_type=MESH
        )

    def other_facet(h):
        return {"facet": h, "vis": j}

    def other_vis(k):
        return {"facet": f, "vis": k}

    def along(q, last_dz):
        return jnp.where(q == 0, 1, jnp.where(q == 1, 3, jnp.where(q == 2, 0, last_dz)))

    def facet_of(p):
        return lax.rem(z + along(p // 2, 2), 4) * 2 + lax.rem(c + lax.rem(p, 2), 2)

    def home_of(p):
        return lax.rem(z + along(p // 2, 0), 4) * 2 + lax.rem(c + lax.rem(p, 2), 2)

    def back(p):
        return jnp.where(p < 2, p + 2, jnp.where(p < 4, p - 2, p))

    def z_first(i):
        return jnp.where(i < 4, 2 * lax.rem(i, 2) + i // 2, i + 1 - 2 * lax.rem(i, 2))

    def two_first(i):
        return jnp.where(i == 0, 2, jnp.where(i == 1, 1, jnp.where(i == 2, 3, 0)))

    load_model = pltpu.make_async_copy(model, image.at[rows(j), :], io.at[0])
    load_observed = pltpu.make_async_copy(observed, obs_v, io.at[1])
    load_small = [
        pltpu.make_async_copy(src, dst, io.at[2 + i])
        for i, (src, dst) in enumerate(((u_hbm, u_off), (v_hbm, v_off), (lists_hbm, lists)))
    ]
    load_model.start()
    for load in load_small:
        load.start()
    load_observed.start()

    flip = c == 1
    first_at = lax.select(flip, j // 4, lax.rem(j, 4))
    second_at = lax.select(flip, lax.rem(j, 4), j // 4)

    def place(da, db):
        a = lax.rem(first_at + da, 4)
        b = lax.rem(second_at + db, 4)
        return lax.select(flip, a * 4 + b, b * 4 + a)

    barrier = pltpu.get_barrier_semaphore()
    for d in range(1, 4):
        pl.semaphore_signal(barrier, inc=1, device_id=other_vis(place(d, 0)), device_id_type=MESH)
        pl.semaphore_signal(barrier, inc=1, device_id=other_vis(place(0, d)), device_id_type=MESH)
    for p in (0, 1, 2, 3, 5):
        pl.semaphore_signal(barrier, inc=1, device_id=other_facet(home_of(p)), device_id_type=MESH)
    pl.semaphore_signal(barrier, inc=1, device_id=other_facet(far), device_id_type=MESH)
    pl.semaphore_wait(barrier, 12)

    def ag_copy(w, da, ta, tb):
        block = image.at[rows(place(da, 0), w), :]
        return remote(
            block, block, ag_ss.at[w, da, ta + 4 * tb], ag_rs.at[w, da, 0 if tb == 0 else 4 - tb]
            if ta == 0 else ag_rs.at[w, 4 - ta, 0], other_vis(place(ta, tb)),
        )

    def ag_wait(w, da, db):
        block = image.at[rows(place(da, db), w), :]
        remote(block, block, ag_ss.at[w, 0, 0], ag_rs.at[w, da, db], other_vis(place(1, 0))).wait_recv()

    def ag_second(w, da):
        for d in (2, 1, 3):
            ag_copy(w, da, 0, d).start()

    def ag_rest(w):
        for db in range(1, 4):
            for da in range(4):
                ag_wait(w, da, db)

    def model_hop(da):
        at = place(da, 0)
        return remote(
            image.at[rows(at), :], image.at[rows(at, 1), :], hop_ss.at[da], hop_rs.at[da], other_facet(far)
        )

    load_model.wait()
    for d in (2, 1, 3):
        ag_copy(0, 0, d, 0).start()
    ag_second(0, 0)
    model_hop(0).start()

    for load in load_small:
        load.wait()

    def listed(h):
        lo, hi = jnp.int32(0), jnp.int32(0)
        for g in range(G):
            hi = jnp.where((lists[0, g] == h) | (lists[1, g] == h), g, hi)
        for g in reversed(range(G)):
            lo = jnp.where((lists[0, g] == h) | (lists[1, g] == h), g, lo)
        return lo, hi

    row = iota((8, LANES), 0)

    @pl.loop(0, 6)
    def _(p):
        tile = jnp.zeros((8, LANES), jnp.int32)
        for half in range(2):
            lo, hi = listed(facet_of(jnp.minimum(p + 2 * half, NF - 1)))
            for at, value in enumerate((u_off[lo], u_off[hi], v_off[lo], v_off[hi])):
                tile = jnp.where(row == 4 * half + at, value, tile)
        uv_out[p] = tile

    def uv_copy(p):
        return remote(uv_out.at[p], uv_in.at[back(p)], uv_ss.at[p], uv_rs.at[back(p)], other_facet(home_of(p)))

    for p in (0, 1, 2, 3, 5):
        uv_copy(p).start()
    uv_in[4] = uv_out[4]

    lane = iota((S, LANES), 1)
    sub = iota((S, LANES), 0)

    @pl.loop(0, XC)
    def _(r):
        for w, facet in enumerate((f, far)):
            co, si = sincos((sub * (facet * STEP + r * LANES + lane)) & (IMG - 1))
            g_c[w, r] = co
            g_s[w, r] = si

    @pl.loop(0, YC)
    def _(r):
        co, si = sincos((sub * (r * LANES + lane)) & (IMG - 1))
        e_c[r] = co
        e_s[r] = si

    for da in (1, 3, 2):
        ag_wait(0, da, 0)
        ag_second(0, da)
        model_hop(da).start()

    for p in (0, 1, 2, 3, 5):
        uv_copy(back(p)).wait_recv()

    y_of = iota((YC, LANES), 0) * LANES + iota((YC, LANES), 1)
    x_of = iota((8, LANES), 0) * LANES + iota((8, LANES), 1)

    @pl.loop(0, 2 * NF)
    def _(n):
        p = n // 2
        w = p // 6
        at = 4 * w + lax.rem(n, 2)
        u = uv_in[p - 2 * w, pl.ds(at, 1), :]
        v = uv_in[p - 2 * w, pl.ds(at + 2, 1), :]
        co, si = sincos((v * y_of) & (IMG - 1))
        pv_c[n] = co
        pv_s[n] = si
        co, si = sincos((u * (x_of + jnp.where(w == 1, far, f) * STEP)) & (IMG - 1))
        pu_c[n] = co
        pu_s[n] = si

    total[...] = jnp.zeros_like(total)

    def p_copy(p, s):
        return remote(
            p_out.at[2 * p + s], p_in.at[2 * back(p) + s],
            p_ss.at[2 * p + s], p_rs.at[2 * back(p) + s], other_facet(home_of(p)),
        )

    def tables(p, s, cv, cu, k):
        n = 2 * p + s
        w = p // 6
        base = 2 * S * s
        for r in range(YC):
            pc = pv_c[n, r : r + 1, :]
            ps = pv_s[n, r : r + 1, :]
            ec, es = e_c[r], e_s[r]
            at = slice(r * LANES, (r + 1) * LANES)
            cv[k, base : base + S, at] = (pc * ec - ps * es).astype(BF16)
            cv[k, base + S : base + 2 * S, at] = (ps * ec + pc * es).astype(BF16)
        for r in range(XC):
            pc = pu_c[n, r : r + 1, :]
            ps = pu_s[n, r : r + 1, :]
            ec, es = g_c[w, r], g_s[w, r]
            at = slice(r * LANES, (r + 1) * LANES)
            cu[2 * k + s, 0:S, at] = (pc * ec - ps * es).astype(BF16)
            cu[2 * k + s, S : 2 * S, at] = (ps * ec + pc * es).astype(BF16)

    def predict(p, window, cv, cu, k):
        t = lax.dot_general(cv[k], image[window, :], NT, preferred_element_type=F32).astype(BF16)
        for s in range(2):
            o = lax.dot_general(
                cu[2 * k + s], t[2 * S * s : 2 * S * (s + 1)], NT, preferred_element_type=F32
            )
            p_out[2 * p + s, 0] = (o[0:S, 0:S] - o[S:, S:]).astype(BF16)
            p_out[2 * p + s, 1] = (-(o[S:, 0:S] + o[0:S, S:])).astype(BF16)

    @pl.loop(0, 4)
    def _(p):
        for s in range(2):
            tables(p, s, cv_a, cu_a, p)

    for da in (0, 1, 3, 2):
        model_hop(da).wait_recv()
        ag_second(1, da)

    @pl.loop(0, 4)
    def _(p):
        for s in range(2):
            tables(p + 4, s, cv_b, cu_b, p)

    ag_rest(0)

    @pl.loop(0, 4)
    def _(i):
        p = z_first(i)

        predict(p, slice(0, FRT), cv_a, cu_a, p)
        for s in range(2):
            p_copy(p, s).start()

    @pl.loop(4, NF)
    def _(i):
        p = jnp.where(i == 4, 5, jnp.where(i == 5, 7, jnp.where(i == 6, 4, 6)))

        @pl.when(i == 5)
        def _():
            ag_rest(1)

        predict(p, pl.ds(pl.multiple_of(p // 6 * FRT, FRT), FRT), cv_b, cu_b, p - 4)

        @pl.when(i < 6)
        def _():
            for s in range(2):
                p_copy(p, s).start()

    @pl.loop(0, NF)
    def _(n):
        for r in range(XC):
            at = slice(r * LANES, (r + 1) * LANES)
            for k in range(2):
                rest = slice(k * S, (k + 1) * S)
                cut[n, at, rest] = cu_a[n, rest, at].T
                cut[NF + n, at, rest] = cu_b[n, rest, at].T

    for n in (8, 9, 12, 13):
        p_in[n] = p_out[n]

    load_observed.wait()
    for p in (0, 1, 2, 3, 5, 7):
        for s in range(2):
            p_copy(back(p), s).wait_recv()

    @pl.loop(0, G)
    def _(g):
        acc = obs_v[g].astype(F32)
        for k in range(2):
            h = lists[k, g]
            slot = jnp.int32(0)
            for e in range(G):
                slot = jnp.where((e < g) & ((lists[0, e] == h) | (lists[1, e] == h)), 1, slot)
            dz = (h // 2 - z) & 3
            q = jnp.where(dz == 0, 2, jnp.where(dz == 1, 0, jnp.where(dz == 2, 3, 1)))
            acc = acc - p_in[4 * q + 2 * ((h - c) & 1) + slot].astype(F32)
        residual[g] = acc.astype(BF16)

    def r_copy(p):
        return remote(
            r_out.at[pl.ds(2 * p, 2)], r_in.at[pl.ds(2 * back(p), 2)],
            r_ss.at[p], r_rs.at[back(p)], other_facet(home_of(p)),
        )

    @pl.loop(0, NF)
    def _(i):
        p = z_first(i)
        lo, hi = listed(facet_of(p))
        r_out[2 * p] = residual[lo]
        r_out[2 * p + 1] = residual[hi]

        @pl.when((i != 5) & (i != 7))
        def _():
            r_copy(p).start()

    for n in (8, 9, 12, 13):
        r_in[n] = r_out[n]

    def d_copy(w, da, db):
        return remote(
            d_out.at[w, db, da], d_in.at[w, 4 - db, da], d_ss.at[w, db, da], d_rs.at[w, 4 - db, da],
            other_vis(place(0, db)),
        )

    def s_copy(da):
        return remote(
            d_out.at[0, 0, da], d_in.at[0, 0, 4 - da], d_ss.at[0, 0, da], d_rs.at[0, 0, 4 - da],
            other_vis(place(da, 0)),
        )

    def image_hop(da):
        return remote(d_out.at[1, 0, da], d_in.at[1, 0, da], up_ss.at[da], up_rs.at[da], other_facet(far))

    def spread(w):
        @pl.loop(0, 12)
        def _(i):
            da = two_first(i // 3)
            db = two_first(lax.rem(i, 3))
            d_out[w, db, da] = total[w, rows(place(da, db)), :].astype(BF16)
            d_copy(w, da, db).start()

    def gathered(w, da):
        acc = total[w, rows(place(da, 0)), :]
        for db in range(1, 4):
            d_copy(w, da, 4 - db).wait_recv()
            acc = acc + d_in[w, db, da].astype(F32)
        return acc

    def both_chips(da):
        acc = gathered(0, da)
        image_hop(da).wait_recv()
        return acc + d_in[1, 0, da].astype(F32)

    def grid(p, w, cv, k):
        zs = []
        for s in range(2):
            re = r_in[2 * p + s, 0]
            im = r_in[2 * p + s, 1]
            top = jnp.concatenate([re, -im], axis=1)
            bottom = jnp.concatenate([-im, -re], axis=1)
            both = jnp.concatenate([top, bottom], axis=0)
            zs.append(lax.dot_general(cut[2 * p + s], both, NN, preferred_element_type=F32).astype(BF16))
        total[w] += lax.dot_general(jnp.concatenate(zs, axis=1), cv[k], NN, preferred_element_type=F32)

    @pl.loop(0, 4)
    def _(i):
        p = jnp.where(i < 2, i + 6, i + 2)

        @pl.when(i == 2)
        def _():
            spread(1)

        @pl.when(lax.rem(i, 2) == 1)
        def _():
            r_copy(p).wait_recv()

        grid(p, jnp.where(i < 2, 1, 0), cv_b, p - 4)

    @pl.loop(0, 4)
    def _(i):
        p = z_first(i)
        r_copy(back(p)).wait_recv()
        grid(p, 0, cv_a, p)

    spread(0)

    @pl.loop(0, 4)
    def _(i):
        da = two_first(i)
        d_out[1, 0, da] = gathered(1, da).astype(BF16)
        image_hop(da).start()

    @pl.loop(0, 3)
    def _(i):
        da = two_first(i)
        d_out[0, 0, da] = both_chips(da).astype(BF16)
        s_copy(da).start()

    acc = both_chips(0)
    for da in (2, 1, 3):
        s_copy(4 - da).wait_recv()
        acc = acc + d_in[0, 0, da].astype(F32)
    dirty[...] = acc * F32(1.0 / (S * S))

    for p in (0, 1, 2, 3, 5):
        uv_copy(p).wait_send()
    for p in (0, 1, 2, 3, 5, 7):
        r_copy(p).wait_send()
        for s in range(2):
            p_copy(p, s).wait_send()
    for da in range(4):
        model_hop(da).wait_send()
        image_hop(da).wait_send()
        for d in range(1, 4):
            for w in range(2):
                ag_copy(w, da, 0, d).wait_send()
                d_copy(w, da, d).wait_send()
    for d in range(1, 4):
        ag_copy(0, 0, d, 0).wait_send()
        s_copy(d).wait_send()


def body(model, observed, u_offsets, v_offsets, facet_lists):
    hbm = pl.BlockSpec(memory_space=pl.ANY)
    vm = pl.BlockSpec(memory_space=pltpu.VMEM)
    dma = pltpu.SemaphoreType.DMA
    return tuple(pl.pallas_call(
            kernel,
            name="major_cycle",
            out_shape=(pltpu.VMEM((ROWS, FW), F32), pltpu.VMEM((G, 2, S, S), BF16)),
            in_specs=[hbm] * 5,
            out_specs=(vm, vm),
            scratch_shapes=[
                pltpu.SMEM((G,), jnp.int32),
                pltpu.SMEM((G,), jnp.int32),
                pltpu.SMEM((2, G), jnp.int32),
                pltpu.VMEM((G, 2, S, S), BF16),
                pltpu.VMEM((2 * FRT, FW), BF16),
                pltpu.VMEM((6, 8, LANES), jnp.int32),
                pltpu.VMEM((6, 8, LANES), jnp.int32),
                pltpu.VMEM((YC, S, LANES), F32),
                pltpu.VMEM((YC, S, LANES), F32),
                pltpu.VMEM((2, XC, S, LANES), F32),
                pltpu.VMEM((2, XC, S, LANES), F32),
                pltpu.VMEM((2 * NF, YC, LANES), F32),
                pltpu.VMEM((2 * NF, YC, LANES), F32),
                pltpu.VMEM((2 * NF, 8, LANES), F32),
                pltpu.VMEM((2 * NF, 8, LANES), F32),
                pltpu.VMEM((4, 4 * S, FW), BF16),
                pltpu.VMEM((4, 4 * S, FW), BF16),
                pltpu.VMEM((NF, 2 * S, FRT), BF16),
                pltpu.VMEM((NF, 2 * S, FRT), BF16),
                pltpu.VMEM((2 * NF, FRT, 2 * S), BF16),
                pltpu.VMEM((2 * NF, 2, S, S), BF16),
                pltpu.VMEM((2 * NF, 2, S, S), BF16),
                pltpu.VMEM((2 * NF, 2, S, S), BF16),
                pltpu.VMEM((2 * NF, 2, S, S), BF16),
                pltpu.VMEM((2, FRT, FW), F32),
                pltpu.VMEM((2, 4, 4, ROWS, FW), BF16),
                pltpu.VMEM((2, 4, 4, ROWS, FW), BF16),
                dma((2, 4, 16)), dma((2, 4, 4)), dma((6,)), dma((6,)), dma((2 * NF,)), dma((2 * NF,)),
                dma((NF,)), dma((NF,)), dma((2, 4, 4)), dma((2, 4, 4)),
                dma((4,)), dma((4,)), dma((4,)), dma((4,)), dma((5,)),
            ],
            compiler_params=pltpu.CompilerParams(
                collective_id=0, has_side_effects=True, vmem_limit_bytes=56 << 20
            ),
        )(model, observed, u_offsets, v_offsets, facet_lists.T))


def solution(mesh):
    in_specs = (
        P(("facet", "vis"), None),
        P(("facet", "vis"), None, None, None),
        P(("facet", "vis")),
        P(("facet", "vis")),
        P(("facet", "vis"), None),
    )
    out_specs = (P(("facet", "vis"), None), P(("facet", "vis"), None, None, None))
    return jax.shard_map(body, mesh=mesh, in_specs=in_specs, out_specs=out_specs, check_vma=False)
```
